256 devices in a mesh: px: 8 (over z_hi, core), py: 32 (over z_lo, x, y).
Axes of the slice: x: 4, y: 4, z: 8 (z_hi: 4, z_lo: 2; z = z_hi * 2 + z_lo), core: 2. Of those that a mesh axis runs over, the one named last changes fastest.
Arguments:
- span: float32 [64, 32, 128, 128], P(None, 'px', 'py'), may hold values from -4 to 4
- potential: float32 [32, 128, 128], P('px', 'py'), may hold values from 0.1 to 2
- cell_matrix: float32 [125, 125], replicated, may hold values from -2 to 7, as said below
- block: bfloat16 [256, 32, 128, 128], P(None, 'px', 'py'), may hold values from -0.015625 to 0.015625
Outputs:
- filtered: float32 [64, 32, 128, 128], P(None, 'px', 'py')
- margin: float32 [64, 256], P('px', 'py')
The draws below stay inside these ranges and needn't reach their ends.
Inputs may be any that keep to these rules, and one draw needn't show every extreme that they name: `cell_matrix`: symmetric.
All inputs are finite; a program needn't handle non-finite values.
Results may differ from the reference program's by a relative error of at most 0.0029.
Values sent between devices are 32-bit elements; how exact they have to be, the bound alone decides.
A program may use at most 128 MiB of HBM per device.

```python
import math
import jax
import jax.numpy as jnp
import numpy as np
from jax import lax

STATES = 64
BLOCK = 256
NZ = 128
NX = 32
NY = 128
NODES = 524288


def lobatto_tables():
    points = np.array([-1.0, -np.sqrt(3.0 / 7.0), 0.0, np.sqrt(3.0 / 7.0), 1.0])
    weights = np.array([0.1, 49.0 / 90.0, 32.0 / 45.0, 49.0 / 90.0, 0.1])
    identity = np.eye(5)
    spacing = points[:, None] - points[None, :] + identity
    barycentric = 1.0 / np.prod(spacing, axis=1)
    derivative = barycentric[None, :] / barycentric[:, None] / spacing * (1.0 - identity)
    derivative = derivative - identity * np.sum(derivative, axis=1)[:, None]
    stiffness = np.dot(derivative.T, weights[:, None] * derivative)
    lumped = identity * weights[None, :]
    along_first = np.kron(np.kron(stiffness, lumped), lumped)
    along_second = np.kron(np.kron(lumped, stiffness), lumped)
    along_third = np.kron(np.kron(lumped, lumped), stiffness)
    return (along_first, along_second, along_third)


def draw_cell_matrix(key, part):
    along_first, along_second, along_third = lobatto_tables()
    coeffs = jnp.exp(jax.random.uniform(jax.random.fold_in(key, 11), (3,), jnp.float32, jnp.log(0.4), jnp.log(0.8)))
    stiff_part = coeffs[0] * jnp.asarray(along_first, jnp.float32)
    stiff_part = stiff_part + coeffs[1] * jnp.asarray(along_second, jnp.float32)
    stiff_part = stiff_part + coeffs[2] * jnp.asarray(along_third, jnp.float32)
    jitter_factor = jax.random.uniform(jax.random.fold_in(key, 12), (125, 125), jnp.float32, -1.0, 1.0)
    jitter_factor = 0.5 * (jitter_factor + jitter_factor.T)
    dense_part = jax.random.uniform(jax.random.fold_in(key, 13), (125, 125), jnp.float32, -1.0, 1.0)
    dense_part = 0.5 * (dense_part + dense_part.T)
    return stiff_part * (1.0 + 0.2 * jitter_factor) + 0.03 * dense_part


def with_spikes(values, rng, source, target, parts, factor):
    owner, partner = [(jnp.arange(values.shape[dim]) // (values.shape[dim] // parts)).reshape([-1 if axis == dim else 1 for axis in range(values.ndim)]) for dim in (source, target)]
    chosen = jax.random.permutation(rng, parts)[partner]
    strong = (owner == chosen) | (owner == (partner + parts // 2) % parts)
    return jnp.where(strong, factor * values, values)


def level_of(rng, shape, split, low, high):
    gain, own = 1.0, jax.random.fold_in(rng, 6)
    for position, shards_of in split:
        draws = jnp.exp(jax.random.uniform(jax.random.fold_in(own, position), (shards_of,), jnp.float32, low / len(split), high / len(split)))
        gain = gain * jnp.repeat(draws, shape[position] // shards_of).reshape([-1 if axis == position else 1 for axis in range(len(shape))])
    return gain


def gaussian(key, extent, deviation, limit, split=(), held_as=jnp.bfloat16):
    loudness = level_of(key, extent, split, -0.22, 0.18) if split else 1.0
    values = jax.random.normal(key, extent, jnp.float32) * deviation * loudness
    return jnp.minimum(jnp.maximum(values, -limit), limit).astype(held_as)


def bell_draw_with(rng, shape, width, most, pieces, heavy, kind=jnp.bfloat16):
    drawn = width * jax.random.normal(rng, shape, jnp.float32)
    if pieces:
        drawn = drawn * level_of(rng, shape, pieces, -0.22, 0.18)
    return jnp.clip(with_spikes(drawn, jax.random.fold_in(rng, 3), *heavy), -most, most).astype(kind)


def setup_inputs(seed: int = 0) -> dict:
    arg_keys = jax.random.split(jax.random.key(seed), 5)
    span = gaussian(arg_keys[0], (STATES, NX, NY, NZ), 0.5, 4.0, ((1, 8), (2, 32)), jnp.float32)
    potential = jnp.clip(jnp.exp(math.log(2.0) - 2.9957323 * jax.random.uniform(arg_keys[1], (NX, NY, NZ), jnp.float32) ** level_of(arg_keys[1], (NX, NY, NZ), ((0, 8), (1, 32)), -0.2, 0.2)), 0.1, 2.0)
    cell_matrix = draw_cell_matrix(jax.random.fold_in(arg_keys[4], 71), 0)
    block = bell_draw_with(arg_keys[3], (BLOCK, NX, NY, NZ), NODES ** -0.5, 0.015625, ((1, 8), (2, 32)), (2, 0, 32, 2.75))
    return dict(span=span, potential=potential, cell_matrix=cell_matrix, block=block)


centre = 13.0
half_width = 9.0


def unfold_cyclic(values, which_axis):
    reordered = jnp.moveaxis(values, which_axis, 0)
    cell_count = reordered.shape[0] // 4
    rest_shape = reordered.shape[1:]
    lower_part = reordered.reshape((cell_count, 4) + rest_shape)
    upper_part = jnp.roll(lower_part[:, 0], -1, axis=0)
    return jnp.concatenate([lower_part, upper_part[:, None]], 1)


def fold_cyclic(values):
    cell_count = values.shape[0]
    rest_shape = values.shape[2:]
    shared = values[:, 0] + jnp.roll(values[:, 4], 1, axis=0)
    joined = jnp.concatenate([shared[:, None], values[:, 1:4]], 1)
    return joined.reshape((4 * cell_count,) + rest_shape)


def cell_products(sectioned, cell_matrix):
    cell_values = jnp.transpose(sectioned, (6, 5, 3, 1, 4, 2, 0))
    shape_cells = cell_values.shape
    flat_cells = cell_values.reshape((shape_cells[0], 125, -1))
    products = jnp.einsum("ij,sjc->sic", cell_matrix, flat_cells, precision=lax.Precision.HIGHEST)
    return jnp.transpose(products.reshape(shape_cells), (4, 1, 5, 2, 6, 3, 0))


def cell_apply(vector, cell_matrix):
    sectioned = unfold_cyclic(vector, 1)
    sectioned = unfold_cyclic(sectioned, 3)
    sectioned = unfold_cyclic(sectioned, 5)
    sectioned = cell_products(sectioned, cell_matrix)
    sectioned = fold_cyclic(sectioned)
    sectioned = fold_cyclic(jnp.moveaxis(sectioned, 0, -1))
    sectioned = fold_cyclic(jnp.moveaxis(sectioned, 0, -1))
    return jnp.moveaxis(sectioned, 0, -1)


def apply_shifted(vector, potential, cell_matrix):
    return cell_apply(vector, cell_matrix) + potential * vector - centre * vector


def filter_states(states, potential, cell_matrix):
    first = apply_shifted(states, potential, cell_matrix) / half_width
    second = 2.0 * apply_shifted(first, potential, cell_matrix) / half_width - states
    return 2.0 * apply_shifted(second, potential, cell_matrix) / half_width - first


def reference(span, potential, cell_matrix, block):
    groups = span.reshape((STATES // 8, 8) + span.shape[1:])

    def run_group(group):
        return filter_states(group, potential, cell_matrix)

    filtered = lax.map(run_group, groups).reshape(span.shape)
    rounded = filtered.astype(jnp.bfloat16).reshape((STATES, -1))
    margin = lax.dot_general(rounded, block.reshape((BLOCK, -1)), (((1,), (1,)), ((), ())), preferred_element_type=jnp.float32)
    return filtered, margin
```

```python
import functools

import jax
import jax.numpy as jnp
from jax import lax
from jax.experimental import pallas as pl
from jax.experimental.pallas import tpu as pltpu
from jax.sharding import PartitionSpec as P

MESH = pl.DeviceIdType.MESH
CENTRE = 13.0
SCALE = 2.0 / 9.0
F32 = jnp.float32
BF16 = jnp.bfloat16
CHUNKS = 2


def rows_to_lanes(parts, width):
    count = len(parts)
    parts = list(parts)
    group = lax.broadcasted_iota(jnp.int32, parts[0].shape, 1) // width
    bit = count // 2
    while bit:
        low = (group & bit) == 0
        for first in range(count):
            if first & bit:
                continue
            a, b = parts[first], parts[first | bit]
            parts[first] = jnp.where(low, a, pltpu.roll(b, bit * width, 1))
            parts[first | bit] = jnp.where(low, pltpu.roll(a, 128 - bit * width, 1), b)
        bit //= 2
    return parts


def kernel(
    px_size, py_size, chunks,
    span_hbm, pot_ref, mat_ref, block_hbm,
    out_hbm, tile_ref,
    span_v, block_v, block_f, block_k, mat_pad, mat3, diag,
    v0, v1, v2, c1, c2, c3, r1, r2, r3,
    out_v, lhs, part, got1, sum1, got2,
    in_sem, out_sem, send_sem, recv_sem, send1, recv1, send2, recv2,
):
    states = 64
    width = states // chunks
    groups = 128 // width
    rows = 128 // groups
    px, py = lax.axis_index("px"), lax.axis_index("py")
    xn, xp = lax.rem(px + 1, px_size), lax.rem(px + px_size - 1, px_size)
    yn, yp = lax.rem(py + 1, py_size), lax.rem(py + py_size - 1, py_size)
    tile_rows = states // px_size
    tile_cols = 256 // py_size
    per_block = 128 // tile_cols

    load_span = pltpu.make_async_copy(span_hbm, span_v, in_sem.at[0])
    load_block = pltpu.make_async_copy(block_hbm, block_v, in_sem.at[1])
    load_span.start()
    load_block.start()

    barrier = pltpu.get_barrier_semaphore()

    def greet(x, y):
        pl.semaphore_signal(barrier, inc=1, device_id=(x, y), device_id_type=MESH)

    for x, y in ((xn, yn), (xn, yp), (xp, yn), (xp, yp)):
        greet(x, y)
    for step in range(1, px_size):
        greet(lax.rem(px + step, px_size), py)

    def greet_y(step, carry):
        greet(px, lax.rem(py + step, py_size))
        return carry

    lax.fori_loop(1, py_size, greet_y, 0)

    def flat(ref, c):
        return ref.at[c].reshape(35 * rows, 128)

    load_span.wait()
    for c in range(chunks):
        for ref in (v0, v1, v2):
            ref[c, 5:7] = jnp.zeros((2, 5, rows, 128), F32)
        for x in range(4):
            for y0 in range(0, 4, groups):
                count = min(groups, 4)
                stack = jnp.concatenate(
                    [span_v[pl.ds(c * width * 16 + x * 4 + y0 + i, width, stride=16), :] for i in range(count)], 0
                )
                turned = stack.T
                pieces = rows_to_lanes([turned[h * rows:(h + 1) * rows] for h in range(groups)], width)
                for i in range(count):
                    v0[c, x, y0 + i] = pieces[i]

    pl.semaphore_wait(barrier, 4 + (px_size - 1) + (py_size - 1))

    def remote(src, dst, c, slot, x, y):
        copy = pltpu.make_async_remote_copy(
            src_ref=src, dst_ref=dst, send_sem=send_sem.at[c, slot], recv_sem=recv_sem.at[c, slot],
            device_id=(x, y), device_id_type=MESH,
        )
        copy.start()
        return copy

    halo, exchange1, exchange2, last = [], [], [], []
    for c in range(chunks):
        halo.append([
            remote(v0.at[c, 0, 0:4], v0.at[c, 4, 0:4], c, 0, xp, py),
            remote(v0.at[c, 0:4, 0], v0.at[c, 0:4, 4], c, 1, px, yp),
            remote(v0.at[c, 0, 0], v0.at[c, 4, 4], c, 2, xp, yp),
        ])

    def exchange(contrib, got, c, base):
        return [
            remote(contrib.at[c, 4, 0:5], got.at[c, 0:5], c, base, xn, py),
            remote(contrib.at[c, 0, 0:5], got.at[c, 5:10], c, base + 1, xp, py),
            remote(contrib.at[c, 0:5, 4], got.at[c, 10:15], c, base + 2, px, yn),
            remote(contrib.at[c, 0:5, 0], got.at[c, 15:20], c, base + 3, px, yp),
            remote(contrib.at[c, 4, 4], got.at[c, 20], c, base + 4, xn, yn),
            remote(contrib.at[c, 4, 0], got.at[c, 21], c, base + 5, xn, yp),
            remote(contrib.at[c, 0, 4], got.at[c, 22], c, base + 6, xp, yn),
            remote(contrib.at[c, 0, 0], got.at[c, 23], c, base + 7, xp, yp),
        ]

    def send_last(c, base):
        return [
            remote(c3.at[c, 4, 0:4], r3.at[c, 0:4], c, base, xn, py),
            remote(c3.at[c, 0:4, 4], r3.at[c, 4:8], c, base + 1, px, yn),
            remote(c3.at[c, 4, 4], r3.at[c, 8], c, base + 2, xn, yn),
        ]

    mat_pad[...] = jnp.zeros((128, 128), F32)
    mat_pad[0:125, 0:125] = mat_ref[...]
    scaled = mat_pad[...] * SCALE
    mat_hi = scaled.astype(BF16)
    mat_lo = (scaled - mat_hi.astype(F32)).astype(BF16)
    i = lax.broadcasted_iota(jnp.int32, (160, 128), 0)
    a = lax.broadcasted_iota(jnp.int32, (160, 128), 1)
    pick = jnp.where((i % 32 < 25) & (a == (i % 32) * 5 + i // 32), 1.0, 0.0).astype(BF16)
    j = lax.broadcasted_iota(jnp.int32, (128, 480), 1)
    b = lax.broadcasted_iota(jnp.int32, (128, 480), 0)
    jj = j % 160
    hit = (jj % 32 < 25) & (b == (jj % 32) * 5 + jj // 32)
    middle = (j >= 160) & (j < 320)
    put_hi = jnp.where(hit & jnp.logical_not(middle), 1.0, 0.0).astype(BF16)
    put_lo = jnp.where(hit & middle, 1.0, 0.0).astype(BF16)
    row_hi = jnp.dot(pick, mat_hi, preferred_element_type=F32).astype(BF16)
    row_lo = jnp.dot(pick, mat_lo, preferred_element_type=F32).astype(BF16)
    mat3[...] = (
        jnp.dot(row_hi, put_hi, preferred_element_type=F32) + jnp.dot(row_lo, put_lo, preferred_element_type=F32)
    ).astype(BF16)

    diag[...] = jnp.zeros((7, 5, rows, 128), F32)
    pot = (jnp.concatenate([pot_ref[...], jnp.zeros((112, 128), F32)], 0) - CENTRE) * SCALE
    pot = pot.T
    lane_group = lax.broadcasted_iota(jnp.int32, (rows, 128), 1) // width
    for x in range(4):
        for y in range(4):
            column = jnp.broadcast_to(pot[:, x * 4 + y:x * 4 + y + 1], (128, 128))
            value = column[0:rows]
            for h in range(1, groups):
                value = jnp.where(lane_group == h, column[h * rows:(h + 1) * rows], value)
            diag[x, y] = value

    load_block.wait()

    def widen(step, carry):
        at = pl.ds(pl.multiple_of(step * 256, 256), 256)
        block_f[at, :] = block_v[at, :].astype(F32)
        return carry

    lax.fori_loop(0, 16, widen, 0)
    for node in range(16):
        block_k[:, node * 128:(node + 1) * 128] = block_f[pl.ds(node, 256, stride=16), :].astype(BF16)

    def apply(source, contrib, c):
        src, dst, dia = flat(source, c), flat(contrib, c), diag.reshape(35 * rows, 128)
        high, low, full = [], [], []
        for r in range(rows):
            full.append(src[pl.ds(r, 32, stride=rows), :])
        full.append(pltpu.roll(full[0], 128 - width, 1))
        for value in full:
            h = value.astype(BF16)
            high.append(h)
            low.append((value - h.astype(F32)).astype(BF16))
        carry = None
        first_row = None
        for k in range(0, rows // 4, 2):
            rhs = jnp.concatenate([
                jnp.concatenate(
                    high[4 * n:4 * n + 5] + high[4 * n:4 * n + 5] + low[4 * n:4 * n + 5], 0
                ) for n in (k, k + 1)
            ], 1)
            product = jnp.dot(mat3[...], rhs, preferred_element_type=F32)
            for n in (0, 1):
                mine = product[:, n * 128:(n + 1) * 128]
                for z in range(4):
                    r = 4 * (k + n) + z
                    value = mine[z * 32:(z + 1) * 32] + dia[pl.ds(r, 32, stride=rows), :] * full[r]
                    if z == 0 and carry is not None:
                        value = value + carry
                    if r == 0:
                        first_row = value
                    else:
                        dst[pl.ds(r, 32, stride=rows), :] = value
                carry = mine[128:160]
        dst[pl.ds(0, 32, stride=rows), :] = first_row + pltpu.roll(carry, width, 1)

    def assemble(contrib, got, c, x, y):
        value = contrib[c, x, y]
        if x == 0:
            value = value + got[c, y]
        if x == 4:
            value = value + got[c, 5 + y]
        if y == 0:
            value = value + got[c, 10 + x]
        if y == 4:
            value = value + got[c, 15 + x]
        corner = {(0, 0): 20, (0, 4): 21, (4, 0): 22, (4, 4): 23}.get((x, y))
        if corner is not None:
            value = value + got[c, corner]
        return value

    for c in range(chunks):
        for copy in halo[c]:
            copy.wait_recv()
        apply(v0, c1, c)
        exchange1.append(exchange(c1, r1, c, 3))
    for c in range(chunks):
        for copy in exchange1[c]:
            copy.wait_recv()
        for x in range(5):
            for y in range(5):
                v1[c, x, y] = 0.5 * assemble(c1, r1, c, x, y)
        apply(v1, c2, c)
        exchange2.append(exchange(c2, r2, c, 11))
    for c in range(chunks):
        for copy in exchange2[c]:
            copy.wait_recv()
        for x in range(5):
            for y in range(5):
                v2[c, x, y] = assemble(c2, r2, c, x, y) - v0[c, x, y]
        apply(v2, c3, c)
        last.append(send_last(c, 19))

    def first_copy(owner):
        return pltpu.make_async_remote_copy(
            src_ref=part.at[owner], dst_ref=got1.at[px], send_sem=send1.at[owner], recv_sem=recv1.at[px],
            device_id=(owner, py), device_id_type=MESH,
        )

    stores = []
    per_chunk = width // tile_rows
    for c in range(chunks):
        for copy in last[c]:
            copy.wait_recv()
        for x in range(4):
            values = []
            for y in range(4):
                value = c3[c, x, y] - v1[c, x, y]
                if x == 0:
                    value = value + r3[c, y]
                if y == 0:
                    value = value + r3[c, 4 + x]
                if x == 0 and y == 0:
                    value = value + r3[c, 8]
                values.append(value)
            for y0 in range(0, 4, groups):
                pieces = rows_to_lanes(values[y0:y0 + groups], width)
                turned = jnp.concatenate(pieces, 0).T
                for i in range(groups):
                    node = x * 4 + y0 + i
                    value = turned[i * width:(i + 1) * width]
                    out_v[pl.ds(c * width * 16 + node, width, stride=16), :] = value
                    lhs[c, :, node * 128:(node + 1) * 128] = value.astype(BF16)
        at = pl.ds(c * width * 16, width * 16)
        store = pltpu.make_async_copy(out_v.at[at], out_hbm.at[at], out_sem.at[c])
        store.start()
        stores.append(store)
        product = lax.dot_general(lhs[c], block_k[...], (((1,), (1,)), ((), ())), preferred_element_type=F32)
        for n in range(per_chunk):
            owner = c * per_chunk + n
            part[owner] = product[n * tile_rows:(n + 1) * tile_rows]

            @pl.when(px != owner)
            def _():
                first_copy(owner).start()

            @pl.when(px == owner)
            def _():
                got1[px] = part[owner]

    for step in range(1, px_size):
        source = lax.rem(px + step, px_size)
        pltpu.make_async_remote_copy(
            src_ref=part.at[0], dst_ref=got1.at[source], send_sem=send1.at[source], recv_sem=recv1.at[source],
            device_id=(source, py), device_id_type=MESH,
        ).wait_recv()
    total = got1[0]
    for n in range(1, px_size):
        total = total + got1[n]
    sum1[0] = total[:, 0:128]
    sum1[1] = total[:, 128:256]

    def second_copy(target):
        return pltpu.make_async_remote_copy(
            src_ref=sum1.at[target // per_block], dst_ref=got2.at[py], send_sem=send2.at[target], recv_sem=recv2.at[py],
            device_id=(px, target), device_id_type=MESH,
        )

    def send_second(step, carry):
        second_copy(lax.rem(py + step, py_size)).start()
        return carry

    lax.fori_loop(1, py_size, send_second, 0)
    got2[py] = sum1[py // per_block]

    def wait_second(step, carry):
        source = lax.rem(py + step, py_size)
        pltpu.make_async_remote_copy(
            src_ref=sum1.at[0], dst_ref=got2.at[source], send_sem=send2.at[source], recv_sem=recv2.at[source],
            device_id=(px, source), device_id_type=MESH,
        ).wait_recv()
        return carry

    lax.fori_loop(1, py_size, wait_second, 0)
    total = got2[0]
    for n in range(1, py_size):
        total = total + got2[n]
    shift = lax.rem(128 - lax.rem(py, per_block) * tile_cols, 128)
    tile_ref[...] = pltpu.roll(total, shift, 1)[:, 0:tile_cols]

    for store in stores:
        store.wait()
    for c in range(chunks):
        for copy in halo[c] + exchange1[c] + exchange2[c] + last[c]:
            copy.wait_send()
    for step in range(1, px_size):
        owner = lax.rem(px + step, px_size)
        first_copy(owner).wait_send()

    def wait_sent(step, carry):
        second_copy(lax.rem(py + step, py_size)).wait_send()
        return carry

    lax.fori_loop(1, py_size, wait_sent, 0)


def local(px_size, py_size, span, potential, cell_matrix, block):
    chunks = CHUNKS
    width = 64 // chunks
    rows = width
    field = pltpu.VMEM((chunks, 7, 5, rows, 128), F32)
    tile = (64 // px_size, 256 // py_size)
    filtered, margin = pl.pallas_call(
        functools.partial(kernel, px_size, py_size, chunks),
        out_shape=(jax.ShapeDtypeStruct((1024, 128), F32), jax.ShapeDtypeStruct(tile, F32)),
        in_specs=[
            pl.BlockSpec(memory_space=pl.ANY),
            pl.BlockSpec(memory_space=pltpu.VMEM),
            pl.BlockSpec(memory_space=pltpu.VMEM),
            pl.BlockSpec(memory_space=pl.ANY),
        ],
        out_specs=(pl.BlockSpec(memory_space=pl.ANY), pl.BlockSpec(memory_space=pltpu.VMEM)),
        scratch_shapes=[
            pltpu.VMEM((1024, 128), F32),
            pltpu.VMEM((4096, 128), BF16),
            pltpu.VMEM((4096, 128), F32),
            pltpu.VMEM((256, 2048), BF16),
            pltpu.VMEM((128, 128), F32),
            pltpu.VMEM((160, 480), BF16),
            pltpu.VMEM((7, 5, rows, 128), F32),
            field, field, field, field, field, field,
            pltpu.VMEM((chunks, 24, rows, 128), F32),
            pltpu.VMEM((chunks, 24, rows, 128), F32),
            pltpu.VMEM((chunks, 9, rows, 128), F32),
            pltpu.VMEM((1024, 128), F32),
            pltpu.VMEM((chunks, width, 2048), BF16),
            pltpu.VMEM((px_size, tile[0], 256), F32),
            pltpu.VMEM((px_size, tile[0], 256), F32),
            pltpu.VMEM((2, tile[0], 128), F32),
            pltpu.VMEM((py_size, tile[0], 128), F32),
            pltpu.SemaphoreType.DMA((2,)),
            pltpu.SemaphoreType.DMA((chunks,)),
            pltpu.SemaphoreType.DMA((chunks, 22)),
            pltpu.SemaphoreType.DMA((chunks, 22)),
            pltpu.SemaphoreType.DMA((px_size,)),
            pltpu.SemaphoreType.DMA((px_size,)),
            pltpu.SemaphoreType.DMA((py_size,)),
            pltpu.SemaphoreType.DMA((py_size,)),
        ],
        compiler_params=pltpu.CompilerParams(
            collective_id=0, has_side_effects=True, vmem_limit_bytes=48 * 1024 * 1024
        ),
    )(span.reshape(1024, 128), potential.reshape(16, 128), cell_matrix, block.reshape(4096, 128))
    return filtered.reshape(span.shape), margin


def solution(mesh):
    in_specs = (P(None, "px", "py", None), P("px", "py", None), P(), P(None, "px", "py", None))
    out_specs = (P(None, "px", "py", None), P("px", "py"))
    body = functools.partial(local, mesh.shape["px"], mesh.shape["py"])
    return jax.shard_map(body, mesh=mesh, in_specs=in_specs, out_specs=out_specs, check_vma=False)
```

```python
import functools

import jax
import jax.numpy as jnp
from jax import lax
from jax.experimental import pallas as pl
from jax.experimental.pallas import tpu as pltpu
from jax.sharding import PartitionSpec as P

MESH = pl.DeviceIdType.MESH
CENTRE = 13.0
SCALE = 2.0 / 9.0
F32 = jnp.float32
BF16 = jnp.bfloat16
CHUNKS = 1
STATES = 64
BLOCK = 256


def rows_to_lanes(parts, width):
    count = len(parts)
    parts = list(parts)
    group = lax.broadcasted_iota(jnp.int32, parts[0].shape, 1) // width
    bit = count // 2
    while bit:
        low = (group & bit) == 0
        for first in range(count):
            if first & bit:
                continue
            a, b = parts[first], parts[first | bit]
            parts[first] = jnp.where(low, a, pltpu.roll(b, bit * width, 1))
            parts[first | bit] = jnp.where(low, pltpu.roll(a, 128 - bit * width, 1), b)
        bit //= 2
    return parts


def kernel(
    px_size, py_size, chunks,
    span_hbm, pot_hbm, mat_hbm, block_hbm,
    out_hbm, tile_ref,
    span_v, mat_v, mat_pad, block_v, block_f, block_k, mat3, diag,
    spans, pots, halo, face_out,
    v0, v1, v2, c1, c2, c3, r1, r2,
    send_back, send_edge, edge, result, lhs, part, got1, sum1, got2,
    ready, local_sem, send_sem, recv_sem, face_send, face_recv, send1, recv1, send2, recv2,
):
    own = STATES // py_size
    per = own // chunks
    width = per * py_size
    groups = 128 // width
    rows = 128 // groups
    px, py = lax.axis_index("px"), lax.axis_index("py")
    xn, xp = lax.rem(px + 1, px_size), lax.rem(px + px_size - 1, px_size)
    tile_rows = STATES // px_size
    tile_cols = BLOCK // py_size
    per_block = 128 // tile_cols

    load_span = pltpu.make_async_copy(span_hbm, span_v, local_sem.at[0])
    load_block = pltpu.make_async_copy(block_hbm, block_v, local_sem.at[1])
    load_mat = pltpu.make_async_copy(mat_hbm, mat_v, local_sem.at[2])
    load_pot = pltpu.make_async_copy(pot_hbm, pots.at[py], local_sem.at[3])
    load_span.start()

    barrier = pltpu.get_barrier_semaphore()

    def greet_y(step, carry):
        pl.semaphore_signal(
            barrier, inc=1, device_id=(px, lax.rem(py + step, py_size)), device_id_type=MESH
        )
        return carry

    def greet_x(step, carry):
        pl.semaphore_signal(
            barrier, inc=1, device_id=(lax.rem(px + step, px_size), py), device_id_type=MESH
        )
        return carry

    lax.fori_loop(1, px_size, greet_x, 0)
    lax.fori_loop(1, py_size, greet_y, 0)
    mat_pad[...] = jnp.zeros((128, 128), F32)
    load_mat.start()
    load_pot.start()
    load_block.start()

    load_span.wait()
    for s in range(own):
        for y in range(4):
            face_out[pl.ds(s * 4 + y, py_size, stride=8), :] = span_v[pl.ds(s * 16 + y, py_size, stride=own * 16), :]

    pl.semaphore_wait(barrier, (px_size - 1) + (py_size - 1))
    for x in (xn, xp):
        pl.semaphore_signal(ready, inc=1, device_id=(x, py), device_id_type=MESH)

    def block_of(ref, index, size):
        return ref.at[pl.ds(pl.multiple_of(index * size, size), size)]

    def send(src, dst, slot, x, y):
        return pltpu.make_async_remote_copy(
            src_ref=src, dst_ref=dst, send_sem=send_sem.at[slot], recv_sem=recv_sem.at[slot],
            device_id=(x, y), device_id_type=MESH,
        )

    def span_copy(target):
        return send(block_of(span_v, target, own * 16), block_of(spans, py, own * 16), 0, px, target)

    def halo_copy(target):
        return send(block_of(face_out, target, 8), block_of(halo, py, 8), 1, xp, target)

    def pot_copy(target):
        return send(pot_hbm, pots.at[py], 2, px, target)

    def over_others(make):
        def body(step, carry):
            make(lax.rem(py + step, py_size)).start()
            return carry

        lax.fori_loop(1, py_size, body, 0)

    def over_all(make):
        def body(step, carry):
            make(lax.rem(py + step, py_size)).start()
            return carry

        lax.fori_loop(0, py_size, body, 0)

    over_others(span_copy)
    pl.semaphore_wait(ready, 2)
    over_all(halo_copy)
    over_others(pot_copy)
    block_of(spans, py, own * 16)[...] = block_of(span_v, py, own * 16)[...]

    load_mat.wait()
    mat_pad[0:125, 0:125] = mat_v[...]
    scaled = mat_pad[...] * SCALE
    mat_hi = scaled.astype(BF16)
    mat_lo = (scaled - mat_hi.astype(F32)).astype(BF16)
    i = lax.broadcasted_iota(jnp.int32, (160, 128), 0)
    a = lax.broadcasted_iota(jnp.int32, (160, 128), 1)
    pick = jnp.where((i % 32 < 25) & (a == (i % 32) * 5 + i // 32), 1.0, 0.0).astype(BF16)
    j = lax.broadcasted_iota(jnp.int32, (128, 480), 1)
    b = lax.broadcasted_iota(jnp.int32, (128, 480), 0)
    jj = j % 160
    hit = (jj % 32 < 25) & (b == (jj % 32) * 5 + jj // 32)
    middle = (j >= 160) & (j < 320)
    put_hi = jnp.where(hit & jnp.logical_not(middle), 1.0, 0.0).astype(BF16)
    put_lo = jnp.where(hit & middle, 1.0, 0.0).astype(BF16)
    row_hi = jnp.dot(pick, mat_hi, preferred_element_type=F32).astype(BF16)
    row_lo = jnp.dot(pick, mat_lo, preferred_element_type=F32).astype(BF16)
    mat3[...] = (
        jnp.dot(row_hi, put_hi, preferred_element_type=F32) + jnp.dot(row_lo, put_lo, preferred_element_type=F32)
    ).astype(BF16)

    for c in range(chunks):
        for ref in (v0, v1, v2):
            ref[c, 5:7] = jnp.zeros((2, 5, rows, 128), F32)

    load_block.wait()

    def widen(step, carry):
        at = pl.ds(pl.multiple_of(step * 256, 256), 256)
        block_f[at, :] = block_v[at, :].astype(F32)
        return carry

    lax.fori_loop(0, BLOCK * 16 // 256, widen, 0)
    for node in range(16):
        block_k[:, node * 128:(node + 1) * 128] = block_f[pl.ds(node, BLOCK, stride=16), :].astype(BF16)

    lane = lax.broadcasted_iota(jnp.int32, (rows, 128), 1)
    first_cell = lax.rem(lane, py_size) == 0
    last_cell = lax.rem(lane, py_size) == py_size - 1

    def from_next(value):
        return jnp.where(last_cell, pltpu.roll(value, py_size - 1, 1), pltpu.roll(value, 127, 1))

    def from_previous(value):
        return jnp.where(first_cell, pltpu.roll(value, 129 - py_size, 1), pltpu.roll(value, 1, 1))

    def turn_in(loads):
        turned = jnp.concatenate(loads, 0).T
        return rows_to_lanes([turned[h * rows:(h + 1) * rows] for h in range(groups)], width)

    def turn_out(values):
        turned = jnp.concatenate(rows_to_lanes(values, width), 0).T
        return [turned[i * width:(i + 1) * width] for i in range(groups)]

    def states_of(ref, c, pitch, per_state, node):
        loads = [
            ref[pl.ds((c * per + s) * per_state + node, py_size, stride=pitch), :] for s in range(per)
        ]
        return jnp.concatenate(loads, 0) if per > 1 else loads[0]

    def flat(ref, c):
        return ref.at[c].reshape(35 * rows, 128)

    def apply(source, contrib, c):
        src, dst = flat(source, c), flat(contrib, c)
        high, low = [], []
        first = None
        for r in range(rows + 1):
            if r < rows:
                value = src[pl.ds(r, 32, stride=rows), :]
                if r == 0:
                    first = value
            else:
                value = pltpu.roll(first, 128 - width, 1)
            h = value.astype(BF16)
            high.append(h)
            low.append((value - h.astype(F32)).astype(BF16))
        carry = None
        first_row = None
        for k in range(0, rows // 4, 2):
            rhs = jnp.concatenate([
                jnp.concatenate(
                    high[4 * n:4 * n + 5] + high[4 * n:4 * n + 5] + low[4 * n:4 * n + 5], 0
                ) for n in (k, k + 1)
            ], 1)
            product = jnp.dot(mat3[...], rhs, preferred_element_type=F32)
            for n in (0, 1):
                mine = product[:, n * 128:(n + 1) * 128]
                for z in range(4):
                    r = 4 * (k + n) + z
                    value = mine[z * 32:(z + 1) * 32]
                    if z == 0 and carry is not None:
                        value = value + carry
                    if r == 0:
                        first_row = value
                    else:
                        dst[pl.ds(r, 32, stride=rows), :] = value
                carry = mine[128:160]
        dst[pl.ds(0, 32, stride=rows), :] = first_row + pltpu.roll(carry, width, 1)

    def folded(contrib, source, c, x, y):
        value = contrib[c, x, y]
        if y == 0:
            value = value + from_previous(contrib[c, x, 4])
        if x < 4:
            value = value + diag[x, y] * source[c, x, y]
        return value

    def face(src, dst, c, slot, x):
        return pltpu.make_async_remote_copy(
            src_ref=src, dst_ref=dst, send_sem=face_send.at[c, slot], recv_sem=face_recv.at[c, slot],
            device_id=(x, py), device_id_type=MESH,
        )

    def send_faces(contrib, source, got, c, base):
        for x in (0, 4):
            for y in range(4):
                contrib[c, x, y] = folded(contrib, source, c, x, y)
        copies = [
            face(contrib.at[c, 4, 0:4], got.at[c, 0], c, base, xn),
            face(contrib.at[c, 0, 0:4], got.at[c, 1], c, base + 1, xp),
        ]
        for copy in copies:
            copy.start()
        return copies

    def place(target, c, x, y, value):
        target[c, x, y] = value
        if y == 0:
            target[c, x, 4] = from_next(value)

    faces = []

    block_wait = pltpu.make_async_remote_copy(
        src_ref=spans.at[pl.ds(0, (py_size - 1) * own * 16)], dst_ref=spans.at[pl.ds(0, (py_size - 1) * own * 16)],
        send_sem=send_sem.at[0], recv_sem=recv_sem.at[0], device_id=(xn, py), device_id_type=MESH,
    )
    halo_wait = pltpu.make_async_remote_copy(
        src_ref=halo, dst_ref=halo, send_sem=send_sem.at[1], recv_sem=recv_sem.at[1],
        device_id=(xn, py), device_id_type=MESH,
    )
    pot_wait = pltpu.make_async_remote_copy(
        src_ref=pots.at[0:py_size - 1], dst_ref=pots.at[0:py_size - 1], send_sem=send_sem.at[2],
        recv_sem=recv_sem.at[2], device_id=(xn, py), device_id_type=MESH,
    )
    block_wait.wait_recv()
    for c in range(chunks):
        for x in range(4):
            for y0 in range(0, 4, groups):
                pieces = turn_in([states_of(spans, c, own * 16, 16, x * 4 + y0 + i) for i in range(groups)])
                for i in range(groups):
                    place(v0, c, x, y0 + i, pieces[i])
    halo_wait.wait_recv()
    for c in range(chunks):
        for y0 in range(0, 4, groups):
            pieces = turn_in([states_of(halo, c, 8, 4, y0 + i) for i in range(groups)])
            for i in range(groups):
                place(v0, c, 4, y0 + i, pieces[i])
        apply(v0, c1, c)
        if c == 0:
            load_pot.wait()
            pot_wait.wait_recv()
            flat_pots = pots.reshape(py_size * 16, 128)
            for x in range(4):
                for y0 in range(0, 4, groups):
                    loads = []
                    for i in range(groups):
                        value = (flat_pots[pl.ds(x * 4 + y0 + i, py_size, stride=16), :] - CENTRE) * SCALE
                        loads += [value] * per
                    pieces = turn_in(loads)
                    for i in range(groups):
                        diag[x, y0 + i] = pieces[i]
        faces.append(send_faces(c1, v0, r1, c, 0))
    for c in range(chunks):
        for x in (1, 2, 3):
            for y in range(4):
                place(v1, c, x, y, 0.5 * folded(c1, v0, c, x, y))

    waiting = faces
    faces = []
    for c in range(chunks):
        for copy in waiting[c]:
            copy.wait_recv()
        for x, n in ((0, 0), (4, 1)):
            for y in range(4):
                place(v1, c, x, y, 0.5 * (c1[c, x, y] + r1[c, n, y]))
        apply(v1, c2, c)
        faces.append(send_faces(c2, v1, r2, c, 2))
    for c in range(chunks):
        for x in (1, 2, 3):
            for y in range(4):
                place(v2, c, x, y, folded(c2, v1, c, x, y) - v0[c, x, y])
    sent = waiting + faces

    waiting = faces
    for c in range(chunks):
        for copy in waiting[c]:
            copy.wait_recv()
        for x, n in ((0, 0), (4, 1)):
            for y in range(4):
                place(v2, c, x, y, c2[c, x, y] + r2[c, n, y] - v0[c, x, y])
        apply(v2, c3, c)
        for x in range(5):
            for y0 in range(0, 4, groups):
                values = []
                for i in range(groups):
                    value = folded(c3, v2, c, x, y0 + i)
                    if x < 4:
                        value = value - v1[c, x, y0 + i]
                    values.append(value)
                pieces = turn_out(values)
                for i in range(groups):
                    for s in range(per):
                        piece = pieces[i][s * py_size:(s + 1) * py_size]
                        state = c * per + s
                        if x < 4:
                            send_back[pl.ds(state * 16 + x * 4 + y0 + i, py_size, stride=own * 16), :] = piece
                        else:
                            send_edge[pl.ds(state * 4 + y0 + i, py_size, stride=8), :] = piece

    def edge_copy(target):
        return send(block_of(send_edge, target, 8), block_of(edge, py, 8), 3, xn, target)

    def back_copy(target):
        return send(block_of(send_back, target, own * 16), block_of(result, py, own * 16), 4, px, target)

    over_all(edge_copy)
    over_others(back_copy)
    block_of(result, py, own * 16)[...] = block_of(send_back, py, own * 16)[...]
    edge_wait = pltpu.make_async_remote_copy(
        src_ref=edge, dst_ref=edge, send_sem=send_sem.at[3], recv_sem=recv_sem.at[3],
        device_id=(xn, py), device_id_type=MESH,
    )
    back_wait = pltpu.make_async_remote_copy(
        src_ref=spans.at[pl.ds(0, (py_size - 1) * own * 16)], dst_ref=result.at[pl.ds(0, (py_size - 1) * own * 16)],
        send_sem=send_sem.at[4], recv_sem=recv_sem.at[4], device_id=(xn, py), device_id_type=MESH,
    )
    edge_wait.wait_recv()
    back_wait.wait_recv()
    for s in range(own):
        for y in range(4):
            at = pl.ds(s * 16 + y, py_size, stride=own * 16)
            result[at, :] = result[at, :] + edge[pl.ds(s * 4 + y, py_size, stride=8), :]
    store = pltpu.make_async_copy(result, out_hbm, local_sem.at[0])
    store.start()
    for node in range(16):
        lhs[:, node * 128:(node + 1) * 128] = result[pl.ds(node, STATES, stride=16), :].astype(BF16)
    product = lax.dot_general(lhs[...], block_k[...], (((1,), (1,)), ((), ())), preferred_element_type=F32)
    for n in range(px_size):
        part[n] = product[n * tile_rows:(n + 1) * tile_rows]

    def first_copy(owner):
        return pltpu.make_async_remote_copy(
            src_ref=part.at[owner], dst_ref=got1.at[px], send_sem=send1, recv_sem=recv1,
            device_id=(owner, py), device_id_type=MESH,
        )

    for step in range(1, px_size):
        first_copy(lax.rem(px + step, px_size)).start()
    got1[px] = part[px]
    first_wait = pltpu.make_async_remote_copy(
        src_ref=part.at[0:px_size - 1], dst_ref=got1.at[0:px_size - 1], send_sem=send1, recv_sem=recv1,
        device_id=(xn, py), device_id_type=MESH,
    )
    first_wait.wait_recv()
    total = got1[0]
    for n in range(1, px_size):
        total = total + got1[n]
    sum1[0] = total[:, 0:128]
    sum1[1] = total[:, 128:256]

    def second_copy(target):
        return pltpu.make_async_remote_copy(
            src_ref=sum1.at[target // per_block], dst_ref=got2.at[py], send_sem=send2, recv_sem=recv2,
            device_id=(px, target), device_id_type=MESH,
        )

    over_others(second_copy)
    got2[py] = sum1[py // per_block]
    second_wait = pltpu.make_async_remote_copy(
        src_ref=got2.at[0:py_size - 1], dst_ref=got2.at[0:py_size - 1], send_sem=send2, recv_sem=recv2,
        device_id=(xn, py), device_id_type=MESH,
    )
    second_wait.wait_recv()
    total = got2[0]
    for n in range(1, py_size):
        total = total + got2[n]
    shift = lax.rem(128 - lax.rem(py, per_block) * tile_cols, 128)
    tile_ref[...] = pltpu.roll(total, shift, 1)[:, 0:tile_cols]

    store.wait()
    for wait in (block_wait, halo_wait, pot_wait, edge_wait, back_wait, first_wait, second_wait):
        wait.wait_send()
    for copies in sent:
        for copy in copies:
            copy.wait_send()


def local(px_size, py_size, span, potential, cell_matrix, block):
    chunks = CHUNKS
    own = STATES // py_size
    width = own // chunks * py_size
    rows = width
    field = pltpu.VMEM((chunks, 7, 5, rows, 128), F32)
    faces = pltpu.VMEM((chunks, 2, 4, rows, 128), F32)
    tile = (STATES // px_size, BLOCK // py_size)
    filtered, margin = pl.pallas_call(
        functools.partial(kernel, px_size, py_size, chunks),
        out_shape=(jax.ShapeDtypeStruct((STATES * 16, 128), F32), jax.ShapeDtypeStruct(tile, F32)),
        in_specs=[pl.BlockSpec(memory_space=pltpu.HBM)] * 4,
        out_specs=(pl.BlockSpec(memory_space=pltpu.HBM), pl.BlockSpec(memory_space=pltpu.VMEM)),
        scratch_shapes=[
            pltpu.VMEM((STATES * 16, 128), F32),
            pltpu.VMEM((125, 125), F32),
            pltpu.VMEM((128, 128), F32),
            pltpu.VMEM((BLOCK * 16, 128), BF16),
            pltpu.VMEM((BLOCK * 16, 128), F32),
            pltpu.VMEM((BLOCK, 2048), BF16),
            pltpu.VMEM((160, 480), BF16),
            pltpu.VMEM((4, 4, rows, 128), F32),
            pltpu.VMEM((STATES * 16, 128), F32),
            pltpu.VMEM((py_size, 16, 128), F32),
            pltpu.VMEM((py_size * 8, 128), F32),
            pltpu.VMEM((py_size * 8, 128), F32),
            field, field, field, field, field, field, faces, faces,
            pltpu.VMEM((STATES * 16, 128), F32),
            pltpu.VMEM((py_size * 8, 128), F32),
            pltpu.VMEM((py_size * 8, 128), F32),
            pltpu.VMEM((STATES * 16, 128), F32),
            pltpu.VMEM((STATES, 2048), BF16),
            pltpu.VMEM((px_size, tile[0], BLOCK), F32),
            pltpu.VMEM((px_size, tile[0], BLOCK), F32),
            pltpu.VMEM((2, tile[0], 128), F32),
            pltpu.VMEM((py_size, tile[0], 128), F32),
            pltpu.SemaphoreType.REGULAR,
            pltpu.SemaphoreType.DMA((4,)),
            pltpu.SemaphoreType.DMA((5,)),
            pltpu.SemaphoreType.DMA((5,)),
            pltpu.SemaphoreType.DMA((chunks, 4)),
            pltpu.SemaphoreType.DMA((chunks, 4)),
            pltpu.SemaphoreType.DMA,
            pltpu.SemaphoreType.DMA,
            pltpu.SemaphoreType.DMA,
            pltpu.SemaphoreType.DMA,
        ],
        compiler_params=pltpu.CompilerParams(
            collective_id=0, has_side_effects=True, vmem_limit_bytes=56 * 1024 * 1024
        ),
    )(span.reshape(STATES * 16, 128), potential.reshape(16, 128), cell_matrix, block.reshape(BLOCK * 16, 128))
    return filtered.reshape(span.shape), margin


def solution(mesh):
    in_specs = (P(None, "px", "py", None), P("px", "py", None), P(), P(None, "px", "py", None))
    out_specs = (P(None, "px", "py", None), P("px", "py"))
    body = functools.partial(local, mesh.shape["px"], mesh.shape["py"])
    return jax.shard_map(body, mesh=mesh, in_specs=in_specs, out_specs=out_specs, check_vma=False)
```

```python
import functools

import jax
import jax.numpy as jnp
from jax import lax
from jax.experimental import pallas as pl
from jax.experimental.pallas import tpu as pltpu
from jax.sharding import PartitionSpec as P

MESH = pl.DeviceIdType.MESH
CENTRE = 13.0
SCALE = 2.0 / 9.0
F32 = jnp.float32
BF16 = jnp.bfloat16
CHUNKS = 2
STATES = 64
BLOCK = 256


def rows_to_lanes(parts, width):
    count = len(parts)
    parts = list(parts)
    group = lax.broadcasted_iota(jnp.int32, parts[0].shape, 1) // width
    bit = count // 2
    while bit:
        low = (group & bit) == 0
        for first in range(count):
            if first & bit:
                continue
            a, b = parts[first], parts[first | bit]
            parts[first] = jnp.where(low, a, pltpu.roll(b, bit * width, 1))
            parts[first | bit] = jnp.where(low, pltpu.roll(a, 128 - bit * width, 1), b)
        bit //= 2
    return parts


def kernel(
    px_size, py_size, chunks,
    span_hbm, pot_hbm, mat_hbm, block_hbm,
    out_hbm, tile_ref,
    span_v, mat_v, mat_pad, block_v, block_f, block_k, mat3, diag,
    spans, pots, halo, face_out,
    v0, v1, v2, c1, c2, c3, r1, r2,
    send_back, send_edge, edge, result, lhs, part, got1, sum1, got2,
    ready, local_sem, send_sem, recv_sem, face_send, face_recv, send1, recv1, send2, recv2,
):
    own = STATES // py_size
    per = own // chunks
    width = per * py_size
    groups = 128 // width
    rows = 128 // groups
    px, py = lax.axis_index("px"), lax.axis_index("py")
    xn, xp = lax.rem(px + 1, px_size), lax.rem(px + px_size - 1, px_size)
    tile_rows = STATES // px_size
    tile_cols = BLOCK // py_size
    per_block = 128 // tile_cols

    load_span = pltpu.make_async_copy(span_hbm, span_v, local_sem.at[0])
    load_block = pltpu.make_async_copy(block_hbm, block_v, local_sem.at[1])
    load_mat = pltpu.make_async_copy(mat_hbm, mat_v, local_sem.at[2])
    load_pot = pltpu.make_async_copy(pot_hbm, pots.at[py], local_sem.at[3])
    load_span.start()

    barrier = pltpu.get_barrier_semaphore()

    def greet_y(step, carry):
        pl.semaphore_signal(
            barrier, inc=1, device_id=(px, lax.rem(py + step, py_size)), device_id_type=MESH
        )
        return carry

    def greet_x(step, carry):
        pl.semaphore_signal(
            barrier, inc=1, device_id=(lax.rem(px + step, px_size), py), device_id_type=MESH
        )
        return carry

    lax.fori_loop(1, px_size, greet_x, 0)
    lax.fori_loop(1, py_size, greet_y, 0)
    mat_pad[...] = jnp.zeros((128, 128), F32)
    load_mat.start()
    load_pot.start()
    load_block.start()

    load_span.wait()
    for s in range(own):
        for y in range(4):
            face_out[pl.ds(s * 4 + y, py_size, stride=8), :] = span_v[pl.ds(s * 16 + y, py_size, stride=own * 16), :]

    pl.semaphore_wait(barrier, (px_size - 1) + (py_size - 1))
    for x in (xn, xp):
        pl.semaphore_signal(ready, inc=1, device_id=(x, py), device_id_type=MESH)

    def block_of(ref, index, size):
        return ref.at[pl.ds(pl.multiple_of(index * size, size), size)]

    def send(src, dst, slot, x, y):
        return pltpu.make_async_remote_copy(
            src_ref=src, dst_ref=dst, send_sem=send_sem.at[slot], recv_sem=recv_sem.at[slot],
            device_id=(x, y), device_id_type=MESH,
        )

    def span_copy(c, target):
        return send(
            block_of(span_v, target * chunks + c, per * 16), block_of(spans.at[c], py, per * 16), 5 + c, px, target
        )

    def halo_copy(target):
        return send(block_of(face_out, target, 8), block_of(halo, py, 8), 1, xp, target)

    def pot_copy(target):
        return send(pot_hbm, pots.at[py], 2, px, target)

    def over_others(make):
        def body(step, carry):
            make(lax.rem(py + step, py_size)).start()
            return carry

        lax.fori_loop(1, py_size, body, 0)

    def over_all(make):
        def body(step, carry):
            make(lax.rem(py + step, py_size)).start()
            return carry

        lax.fori_loop(0, py_size, body, 0)

    over_others(functools.partial(span_copy, 0))
    pl.semaphore_wait(ready, 2)
    over_all(halo_copy)
    for c in range(1, chunks):
        over_others(functools.partial(span_copy, c))
    for c in range(chunks):
        block_of(spans.at[c], py, per * 16)[...] = block_of(span_v, py * chunks + c, per * 16)[...]

    load_mat.wait()
    mat_pad[0:125, 0:125] = mat_v[...]
    scaled = mat_pad[...] * SCALE
    mat_hi = scaled.astype(BF16)
    mat_lo = (scaled - mat_hi.astype(F32)).astype(BF16)
    i = lax.broadcasted_iota(jnp.int32, (160, 128), 0)
    a = lax.broadcasted_iota(jnp.int32, (160, 128), 1)
    pick = jnp.where((i % 32 < 25) & (a == (i % 32) * 5 + i // 32), 1.0, 0.0).astype(BF16)
    j = lax.broadcasted_iota(jnp.int32, (128, 480), 1)
    b = lax.broadcasted_iota(jnp.int32, (128, 480), 0)
    jj = j % 160
    hit = (jj % 32 < 25) & (b == (jj % 32) * 5 + jj // 32)
    middle = (j >= 160) & (j < 320)
    put_hi = jnp.where(hit & jnp.logical_not(middle), 1.0, 0.0).astype(BF16)
    put_lo = jnp.where(hit & middle, 1.0, 0.0).astype(BF16)
    row_hi = jnp.dot(pick, mat_hi, preferred_element_type=F32).astype(BF16)
    row_lo = jnp.dot(pick, mat_lo, preferred_element_type=F32).astype(BF16)
    mat3[...] = (
        jnp.dot(row_hi, put_hi, preferred_element_type=F32) + jnp.dot(row_lo, put_lo, preferred_element_type=F32)
    ).astype(BF16)

    for c in range(chunks):
        for ref in (v0, v1, v2):
            ref[c, 5:7] = jnp.zeros((2, 5, rows, 128), F32)

    load_block.wait()

    def widen(step, carry):
        at = pl.ds(pl.multiple_of(step * 256, 256), 256)
        block_f[at, :] = block_v[at, :].astype(F32)
        return carry

    lax.fori_loop(0, BLOCK * 16 // 256, widen, 0)
    for node in range(16):
        block_k[:, node * 128:(node + 1) * 128] = block_f[pl.ds(node, BLOCK, stride=16), :].astype(BF16)

    over_others(pot_copy)

    lane = lax.broadcasted_iota(jnp.int32, (rows, 128), 1)
    first_cell = lax.rem(lane, py_size) == 0
    last_cell = lax.rem(lane, py_size) == py_size - 1

    def from_next(value):
        return jnp.where(last_cell, pltpu.roll(value, py_size - 1, 1), pltpu.roll(value, 127, 1))

    def from_previous(value):
        return jnp.where(first_cell, pltpu.roll(value, 129 - py_size, 1), pltpu.roll(value, 1, 1))

    def turn_in(loads):
        turned = jnp.concatenate(loads, 0).T
        return rows_to_lanes([turned[h * rows:(h + 1) * rows] for h in range(groups)], width)

    def turn_out(values):
        turned = jnp.concatenate(rows_to_lanes(values, width), 0).T
        return [turned[i * width:(i + 1) * width] for i in range(groups)]

    def states_of(ref, first, pitch):
        loads = [ref[pl.ds(start, py_size, stride=pitch), :] for start in first]
        return jnp.concatenate(loads, 0) if per > 1 else loads[0]

    def flat(ref, c):
        return ref.at[c].reshape(35 * rows, 128)

    def apply(source, contrib, c):
        src, dst = flat(source, c), flat(contrib, c)
        high, low = [], []
        first = None
        for r in range(rows + 1):
            if r < rows:
                value = src[pl.ds(r, 32, stride=rows), :]
                if r == 0:
                    first = value
            else:
                value = pltpu.roll(first, 128 - width, 1)
            h = value.astype(BF16)
            high.append(h)
            low.append((value - h.astype(F32)).astype(BF16))
        carry = None
        first_row = None
        for k in range(0, rows // 4, 2):
            rhs = jnp.concatenate([
                jnp.concatenate(
                    high[4 * n:4 * n + 5] + high[4 * n:4 * n + 5] + low[4 * n:4 * n + 5], 0
                ) for n in (k, k + 1)
            ], 1)
            product = jnp.dot(mat3[...], rhs, preferred_element_type=F32)
            for n in (0, 1):
                mine = product[:, n * 128:(n + 1) * 128]
                for z in range(4):
                    r = 4 * (k + n) + z
                    value = mine[z * 32:(z + 1) * 32]
                    if z == 0 and carry is not None:
                        value = value + carry
                    if r == 0:
                        first_row = value
                    else:
                        dst[pl.ds(r, 32, stride=rows), :] = value
                carry = mine[128:160]
        dst[pl.ds(0, 32, stride=rows), :] = first_row + pltpu.roll(carry, width, 1)

    def folded(contrib, source, c, x, y):
        value = contrib[c, x, y]
        if y == 0:
            value = value + from_previous(contrib[c, x, 4])
        if x < 4:
            value = value + diag[x, y] * source[c, x, y]
        return value

    def face(src, dst, c, slot, x):
        return pltpu.make_async_remote_copy(
            src_ref=src, dst_ref=dst, send_sem=face_send.at[c, slot], recv_sem=face_recv.at[c, slot],
            device_id=(x, py), device_id_type=MESH,
        )

    def send_faces(contrib, source, got, c, base):
        for x in (0, 4):
            for y in range(4):
                contrib[c, x, y] = folded(contrib, source, c, x, y)
        copies = [
            face(contrib.at[c, 4, 0:4], got.at[c, 0], c, base, xn),
            face(contrib.at[c, 0, 0:4], got.at[c, 1], c, base + 1, xp),
        ]
        for copy in copies:
            copy.start()
        return copies

    def place(target, c, x, y, value):
        target[c, x, y] = value
        if y == 0:
            target[c, x, 4] = from_next(value)

    faces = []

    others = pl.ds(0, (py_size - 1) * per * 16)
    block_waits = [
        pltpu.make_async_remote_copy(
            src_ref=spans.at[c, others], dst_ref=spans.at[c, others],
            send_sem=send_sem.at[5 + c], recv_sem=recv_sem.at[5 + c], device_id=(xn, py), device_id_type=MESH,
        ) for c in range(chunks)
    ]
    halo_wait = pltpu.make_async_remote_copy(
        src_ref=halo, dst_ref=halo, send_sem=send_sem.at[1], recv_sem=recv_sem.at[1],
        device_id=(xn, py), device_id_type=MESH,
    )
    pot_wait = pltpu.make_async_remote_copy(
        src_ref=pots.at[0:py_size - 1], dst_ref=pots.at[0:py_size - 1], send_sem=send_sem.at[2],
        recv_sem=recv_sem.at[2], device_id=(xn, py), device_id_type=MESH,
    )
    for c in range(chunks):
        block_waits[c].wait_recv()
        for x in range(4):
            for y0 in range(0, 4, groups):
                pieces = turn_in([
                    states_of(spans.at[c], [s * 16 + x * 4 + y0 + i for s in range(per)], per * 16)
                    for i in range(groups)
                ])
                for i in range(groups):
                    place(v0, c, x, y0 + i, pieces[i])
        if c == 0:
            halo_wait.wait_recv()
        for y0 in range(0, 4, groups):
            pieces = turn_in([
                states_of(halo, [(c * per + s) * 4 + y0 + i for s in range(per)], 8) for i in range(groups)
            ])
            for i in range(groups):
                place(v0, c, 4, y0 + i, pieces[i])
        apply(v0, c1, c)
        if c == 0:
            load_pot.wait()
            pot_wait.wait_recv()
            flat_pots = pots.reshape(py_size * 16, 128)
            for x in range(4):
                for y0 in range(0, 4, groups):
                    loads = []
                    for i in range(groups):
                        value = (flat_pots[pl.ds(x * 4 + y0 + i, py_size, stride=16), :] - CENTRE) * SCALE
                        loads += [value] * per
                    pieces = turn_in(loads)
                    for i in range(groups):
                        diag[x, y0 + i] = pieces[i]
        faces.append(send_faces(c1, v0, r1, c, 0))
    for c in range(chunks):
        for x in (1, 2, 3):
            for y in range(4):
                place(v1, c, x, y, 0.5 * folded(c1, v0, c, x, y))

    waiting = faces
    faces = []
    for c in range(chunks):
        for copy in waiting[c]:
            copy.wait_recv()
        for x, n in ((0, 0), (4, 1)):
            for y in range(4):
                place(v1, c, x, y, 0.5 * (c1[c, x, y] + r1[c, n, y]))
        apply(v1, c2, c)
        faces.append(send_faces(c2, v1, r2, c, 2))
    for c in range(chunks):
        for x in (1, 2, 3):
            for y in range(4):
                place(v2, c, x, y, folded(c2, v1, c, x, y) - v0[c, x, y])
    sent = waiting + faces

    def edge_copy(target):
        return send(block_of(send_edge, target, 8), block_of(edge, py, 8), 3, xn, target)

    def back_copy(c, target):
        return send(
            block_of(send_back.at[c], target, per * 16), block_of(result, py * chunks + c, per * 16),
            5 + chunks + c, px, target,
        )

    waiting = faces
    for c in range(chunks):
        for copy in waiting[c]:
            copy.wait_recv()
        for x, n in ((0, 0), (4, 1)):
            for y in range(4):
                place(v2, c, x, y, c2[c, x, y] + r2[c, n, y] - v0[c, x, y])
        apply(v2, c3, c)
        for x in range(5):
            for y0 in range(0, 4, groups):
                values = []
                for i in range(groups):
                    value = folded(c3, v2, c, x, y0 + i)
                    if x < 4:
                        value = value - v1[c, x, y0 + i]
                    values.append(value)
                pieces = turn_out(values)
                for i in range(groups):
                    for s in range(per):
                        piece = pieces[i][s * py_size:(s + 1) * py_size]
                        state = c * per + s
                        if x < 4:
                            send_back[c, pl.ds(s * 16 + x * 4 + y0 + i, py_size, stride=per * 16), :] = piece
                        else:
                            send_edge[pl.ds(state * 4 + y0 + i, py_size, stride=8), :] = piece

        if c == chunks - 1:
            over_all(edge_copy)
        over_others(functools.partial(back_copy, c))
        block_of(result, py * chunks + c, per * 16)[...] = block_of(send_back.at[c], py, per * 16)[...]

    edge_wait = pltpu.make_async_remote_copy(
        src_ref=edge, dst_ref=edge, send_sem=send_sem.at[3], recv_sem=recv_sem.at[3],
        device_id=(xn, py), device_id_type=MESH,
    )
    back_waits = [
        pltpu.make_async_remote_copy(
            src_ref=send_back.at[c, others], dst_ref=result.at[others],
            send_sem=send_sem.at[5 + chunks + c], recv_sem=recv_sem.at[5 + chunks + c],
            device_id=(xn, py), device_id_type=MESH,
        ) for c in range(chunks)
    ]
    edge_wait.wait_recv()
    for wait in back_waits:
        wait.wait_recv()
    for s in range(own):
        for y in range(4):
            at = pl.ds(s * 16 + y, py_size, stride=own * 16)
            result[at, :] = result[at, :] + edge[pl.ds(s * 4 + y, py_size, stride=8), :]
    store = pltpu.make_async_copy(result, out_hbm, local_sem.at[0])
    store.start()
    for node in range(16):
        lhs[:, node * 128:(node + 1) * 128] = result[pl.ds(node, STATES, stride=16), :].astype(BF16)
    product = lax.dot_general(lhs[...], block_k[...], (((1,), (1,)), ((), ())), preferred_element_type=F32)
    for n in range(px_size):
        part[n] = product[n * tile_rows:(n + 1) * tile_rows]

    def first_copy(owner):
        return pltpu.make_async_remote_copy(
            src_ref=part.at[owner], dst_ref=got1.at[px], send_sem=send1, recv_sem=recv1,
            device_id=(owner, py), device_id_type=MESH,
        )

    for step in range(1, px_size):
        first_copy(lax.rem(px + step, px_size)).start()
    got1[px] = part[px]
    first_wait = pltpu.make_async_remote_copy(
        src_ref=part.at[0:px_size - 1], dst_ref=got1.at[0:px_size - 1], send_sem=send1, recv_sem=recv1,
        device_id=(xn, py), device_id_type=MESH,
    )
    first_wait.wait_recv()
    total = got1[0]
    for n in range(1, px_size):
        total = total + got1[n]
    sum1[0] = total[:, 0:128]
    sum1[1] = total[:, 128:256]

    def second_copy(target):
        return pltpu.make_async_remote_copy(
            src_ref=sum1.at[target // per_block], dst_ref=got2.at[py], send_sem=send2, recv_sem=recv2,
            device_id=(px, target), device_id_type=MESH,
        )

    over_others(second_copy)
    got2[py] = sum1[py // per_block]
    second_wait = pltpu.make_async_remote_copy(
        src_ref=got2.at[0:py_size - 1], dst_ref=got2.at[0:py_size - 1], send_sem=send2, recv_sem=recv2,
        device_id=(xn, py), device_id_type=MESH,
    )
    second_wait.wait_recv()
    total = got2[0]
    for n in range(1, py_size):
        total = total + got2[n]
    shift = lax.rem(128 - lax.rem(py, per_block) * tile_cols, 128)
    tile_ref[...] = pltpu.roll(total, shift, 1)[:, 0:tile_cols]

    store.wait()
    for wait in block_waits + [halo_wait, pot_wait, edge_wait] + back_waits + [first_wait, second_wait]:
        wait.wait_send()
    for copies in sent:
        for copy in copies:
            copy.wait_send()


def local(px_size, py_size, span, potential, cell_matrix, block):
    chunks = CHUNKS
    own = STATES // py_size
    width = own // chunks * py_size
    rows = width
    field = pltpu.VMEM((chunks, 7, 5, rows, 128), F32)
    faces = pltpu.VMEM((chunks, 2, 4, rows, 128), F32)
    tile = (STATES // px_size, BLOCK // py_size)
    filtered, margin = pl.pallas_call(
        functools.partial(kernel, px_size, py_size, chunks),
        out_shape=(jax.ShapeDtypeStruct((STATES * 16, 128), F32), jax.ShapeDtypeStruct(tile, F32)),
        in_specs=[pl.BlockSpec(memory_space=pltpu.HBM)] * 4,
        out_specs=(pl.BlockSpec(memory_space=pl.ANY), pl.BlockSpec(memory_space=pltpu.VMEM)),
        scratch_shapes=[
            pltpu.VMEM((STATES * 16, 128), F32),
            pltpu.VMEM((125, 125), F32),
            pltpu.VMEM((128, 128), F32),
            pltpu.VMEM((BLOCK * 16, 128), BF16),
            pltpu.VMEM((BLOCK * 16, 128), F32),
            pltpu.VMEM((BLOCK, 2048), BF16),
            pltpu.VMEM((160, 480), BF16),
            pltpu.VMEM((4, 4, rows, 128), F32),
            pltpu.VMEM((chunks, STATES * 16 // chunks, 128), F32),
            pltpu.VMEM((py_size, 16, 128), F32),
            pltpu.VMEM((py_size * 8, 128), F32),
            pltpu.VMEM((py_size * 8, 128), F32),
            field, field, field, field, field, field, faces, faces,
            pltpu.VMEM((chunks, STATES * 16 // chunks, 128), F32),
            pltpu.VMEM((py_size * 8, 128), F32),
            pltpu.VMEM((py_size * 8, 128), F32),
            pltpu.VMEM((STATES * 16, 128), F32),
            pltpu.VMEM((STATES, 2048), BF16),
            pltpu.VMEM((px_size, tile[0], BLOCK), F32),
            pltpu.VMEM((px_size, tile[0], BLOCK), F32),
            pltpu.VMEM((2, tile[0], 128), F32),
            pltpu.VMEM((py_size, tile[0], 128), F32),
            pltpu.SemaphoreType.REGULAR,
            pltpu.SemaphoreType.DMA((4,)),
            pltpu.SemaphoreType.DMA((5 + 2 * chunks,)),
            pltpu.SemaphoreType.DMA((5 + 2 * chunks,)),
            pltpu.SemaphoreType.DMA((chunks, 4)),
            pltpu.SemaphoreType.DMA((chunks, 4)),
            pltpu.SemaphoreType.DMA,
            pltpu.SemaphoreType.DMA,
            pltpu.SemaphoreType.DMA,
            pltpu.SemaphoreType.DMA,
        ],
        compiler_params=pltpu.CompilerParams(
            collective_id=0, has_side_effects=True, vmem_limit_bytes=40 * 1024 * 1024
        ),
    )(*(pltpu.with_memory_space_constraint(value, pltpu.HBM) for value in (
        span.reshape(STATES * 16, 128), potential.reshape(16, 128), cell_matrix, block.reshape(BLOCK * 16, 128)
    )))
    return filtered.reshape(span.shape), margin


def solution(mesh):
    in_specs = (P(None, "px", "py", None), P("px", "py", None), P(), P(None, "px", "py", None))
    out_specs = (P(None, "px", "py", None), P("px", "py"))
    body = functools.partial(local, mesh.shape["px"], mesh.shape["py"])
    return jax.shard_map(body, mesh=mesh, in_specs=in_specs, out_specs=out_specs, check_vma=False)
```

```python
import functools

import jax
import jax.numpy as jnp
from jax import lax
from jax.experimental import pallas as pl
from jax.experimental.pallas import tpu as pltpu
from jax.sharding import PartitionSpec as P

MESH = pl.DeviceIdType.MESH
CENTRE = 13.0
SCALE = 2.0 / 9.0
F32 = jnp.float32
BF16 = jnp.bfloat16
CHUNKS = 2
STATES = 64
BLOCK = 256


def rows_to_lanes(parts, width):
    count = len(parts)
    parts = list(parts)
    group = lax.broadcasted_iota(jnp.int32, parts[0].shape, 1) // width
    bit = count // 2
    while bit:
        low = (group & bit) == 0
        for first in range(count):
            if first & bit:
                continue
            a, b = parts[first], parts[first | bit]
            parts[first] = jnp.where(low, a, pltpu.roll(b, bit * width, 1))
            parts[first | bit] = jnp.where(low, pltpu.roll(a, 128 - bit * width, 1), b)
        bit //= 2
    return parts


def kernel(
    px_size, py_size, chunks,
    span_hbm, pot_hbm, mat_hbm, block_hbm,
    out_hbm, tile_ref,
    span_v, mat_v, mat_pad, block_v, block_f, block_k, mat3, diag,
    spans, pots, halo, face_out,
    v0, v1, v2, c1, c2, c3, r1, r2,
    send_back, send_edge, edge, result, lhs, part, got1, sum1, got2,
    ready, local_sem, send_sem, recv_sem, face_send, face_recv, send1, recv1, send2, recv2,
):
    own = STATES // py_size
    per = own // chunks
    width = per * py_size
    groups = 128 // width
    rows = 128 // groups
    px, py = lax.axis_index("px"), lax.axis_index("py")
    xn, xp = lax.rem(px + 1, px_size), lax.rem(px + px_size - 1, px_size)
    tile_rows = STATES // px_size
    tile_cols = BLOCK // py_size
    per_block = 128 // tile_cols

    load_span = pltpu.make_async_copy(span_hbm, span_v, local_sem.at[0])
    load_block = pltpu.make_async_copy(block_hbm, block_v, local_sem.at[1])
    load_mat = pltpu.make_async_copy(mat_hbm, mat_v, local_sem.at[2])
    load_pot = pltpu.make_async_copy(pot_hbm, pots.at[py], local_sem.at[3])
    load_span.start()

    barrier = pltpu.get_barrier_semaphore()

    z_part = [lax.rem(py // 16 + n, 2) * 16 for n in range(2)]
    x_part = [lax.rem(lax.rem(py // 4, 4) + n, 4) * 4 for n in range(4)]
    y_part = [lax.rem(lax.rem(py, 4) + n, 4) for n in range(4)]
    offsets = [(z, x, y) for z in range(2) for x in range(4) for y in range(4)]
    offsets.sort(key=lambda o: -(o[0] + min(o[1], 4 - o[1]) + min(o[2], 4 - o[2])))
    group = [z_part[z] + x_part[x] + y_part[y] for z, x, y in offsets]
    steps = sorted(range(1, px_size), key=lambda n: -min(n, px_size - n))
    others_x = [lax.rem(px + n, px_size) for n in steps]

    for x in others_x:
        pl.semaphore_signal(barrier, inc=1, device_id=(x, py), device_id_type=MESH)
    for y in group[:-1]:
        pl.semaphore_signal(barrier, inc=1, device_id=(px, y), device_id_type=MESH)
    mat_pad[...] = jnp.zeros((128, 128), F32)
    load_mat.start()
    load_pot.start()
    load_block.start()

    load_span.wait()
    for s in range(own):
        for y in range(4):
            face_out[pl.ds(s * 4 + y, py_size, stride=8), :] = span_v[pl.ds(s * 16 + y, py_size, stride=own * 16), :]

    pl.semaphore_wait(barrier, (px_size - 1) + (py_size - 1))
    for x in (xn, xp):
        pl.semaphore_signal(ready, inc=1, device_id=(x, py), device_id_type=MESH)

    def block_of(ref, index, size):
        return ref.at[pl.ds(pl.multiple_of(index * size, size), size)]

    def send(src, dst, slot, x, y):
        return pltpu.make_async_remote_copy(
            src_ref=src, dst_ref=dst, send_sem=send_sem.at[slot], recv_sem=recv_sem.at[slot],
            device_id=(x, y), device_id_type=MESH,
        )

    def span_copy(c, target):
        return send(
            block_of(span_v, target * chunks + c, per * 16), block_of(spans.at[c], py, per * 16), 5 + c, px, target
        )

    def halo_copy(target):
        return send(block_of(face_out, target, 8), block_of(halo, py, 8), 1, xp, target)

    def pot_copy(first, target):
        at = pl.ds(0, 4) if first else pl.ds(4, 12)
        return send(pot_hbm.at[at], pots.at[py, at], 0 if first else 2, px, target)

    def over_others(make):
        for target in group[:-1]:
            make(target).start()

    def over_all(make):
        for target in group:
            make(target).start()

    over_others(functools.partial(span_copy, 0))
    over_others(functools.partial(pot_copy, True))
    pl.semaphore_wait(ready, 2)
    over_all(halo_copy)
    for c in range(1, chunks):
        over_others(functools.partial(span_copy, c))
    for c in range(chunks):
        block_of(spans.at[c], py, per * 16)[...] = block_of(span_v, py * chunks + c, per * 16)[...]

    load_mat.wait()
    mat_pad[0:125, 0:125] = mat_v[...]
    scaled = mat_pad[...] * SCALE
    mat_hi = scaled.astype(BF16)
    mat_lo = (scaled - mat_hi.astype(F32)).astype(BF16)
    i = lax.broadcasted_iota(jnp.int32, (160, 128), 0)
    a = lax.broadcasted_iota(jnp.int32, (160, 128), 1)
    pick = jnp.where((i % 32 < 25) & (a == (i % 32) * 5 + i // 32), 1.0, 0.0).astype(BF16)
    j = lax.broadcasted_iota(jnp.int32, (128, 480), 1)
    b = lax.broadcasted_iota(jnp.int32, (128, 480), 0)
    jj = j % 160
    hit = (jj % 32 < 25) & (b == (jj % 32) * 5 + jj // 32)
    middle = (j >= 160) & (j < 320)
    put_hi = jnp.where(hit & jnp.logical_not(middle), 1.0, 0.0).astype(BF16)
    put_lo = jnp.where(hit & middle, 1.0, 0.0).astype(BF16)
    row_hi = jnp.dot(pick, mat_hi, preferred_element_type=F32).astype(BF16)
    row_lo = jnp.dot(pick, mat_lo, preferred_element_type=F32).astype(BF16)
    mat3[...] = (
        jnp.dot(row_hi, put_hi, preferred_element_type=F32) + jnp.dot(row_lo, put_lo, preferred_element_type=F32)
    ).astype(BF16)

    for c in range(chunks):
        for ref in (v0, v1, v2):
            ref[c, 5:7] = jnp.zeros((2, 5, rows, 128), F32)

    load_block.wait()

    def widen(step, carry):
        at = pl.ds(pl.multiple_of(step * 256, 256), 256)
        block_f[at, :] = block_v[at, :].astype(F32)
        return carry

    lax.fori_loop(0, BLOCK * 16 // 256, widen, 0)
    for node in range(16):
        block_k[:, node * 128:(node + 1) * 128] = block_f[pl.ds(node, BLOCK, stride=16), :].astype(BF16)

    over_others(functools.partial(pot_copy, False))

    lane = lax.broadcasted_iota(jnp.int32, (rows, 128), 1)
    first_cell = lax.rem(lane, py_size) == 0
    last_cell = lax.rem(lane, py_size) == py_size - 1

    def from_next(value):
        return jnp.where(last_cell, pltpu.roll(value, py_size - 1, 1), pltpu.roll(value, 127, 1))

    def from_previous(value):
        return jnp.where(first_cell, pltpu.roll(value, 129 - py_size, 1), pltpu.roll(value, 1, 1))

    def turn_in(loads):
        turned = jnp.concatenate(loads, 0).T
        return rows_to_lanes([turned[h * rows:(h + 1) * rows] for h in range(groups)], width)

    def turn_out(values):
        turned = jnp.concatenate(rows_to_lanes(values, width), 0).T
        return [turned[i * width:(i + 1) * width] for i in range(groups)]

    def states_of(ref, first, pitch):
        loads = [ref[pl.ds(start, py_size, stride=pitch), :] for start in first]
        return jnp.concatenate(loads, 0) if per > 1 else loads[0]

    def flat(ref, c):
        return ref.at[c].reshape(35 * rows, 128)

    def apply(source, contrib, c):
        src, dst = flat(source, c), flat(contrib, c)
        high, low = [], []
        first = None
        for r in range(rows + 1):
            if r < rows:
                value = src[pl.ds(r, 32, stride=rows), :]
                if r == 0:
                    first = value
            else:
                value = pltpu.roll(first, 128 - width, 1)
            h = value.astype(BF16)
            high.append(h)
            low.append((value - h.astype(F32)).astype(BF16))
        carry = None
        first_row = None
        for k in range(0, rows // 4, 2):
            rhs = jnp.concatenate([
                jnp.concatenate(
                    high[4 * n:4 * n + 5] + high[4 * n:4 * n + 5] + low[4 * n:4 * n + 5], 0
                ) for n in (k, k + 1)
            ], 1)
            product = jnp.dot(mat3[...], rhs, preferred_element_type=F32)
            for n in (0, 1):
                mine = product[:, n * 128:(n + 1) * 128]
                for z in range(4):
                    r = 4 * (k + n) + z
                    value = mine[z * 32:(z + 1) * 32]
                    if z == 0 and carry is not None:
                        value = value + carry
                    if r == 0:
                        first_row = value
                    else:
                        dst[pl.ds(r, 32, stride=rows), :] = value
                carry = mine[128:160]
        dst[pl.ds(0, 32, stride=rows), :] = first_row + pltpu.roll(carry, width, 1)

    def folded(contrib, source, c, x, y):
        value = contrib[c, x, y]
        if y == 0:
            value = value + from_previous(contrib[c, x, 4])
        if x < 4:
            value = value + diag[x, y] * source[c, x, y]
        return value

    def face(src, dst, c, slot, x):
        return pltpu.make_async_remote_copy(
            src_ref=src, dst_ref=dst, send_sem=face_send.at[c, slot], recv_sem=face_recv.at[c, slot],
            device_id=(x, py), device_id_type=MESH,
        )

    def send_faces(contrib, source, got, c, base):
        for x in (0, 4):
            for y in range(4):
                contrib[c, x, y] = folded(contrib, source, c, x, y)
        copies = [
            face(contrib.at[c, 4, 0:4], got.at[c, 0], c, base, xn),
            face(contrib.at[c, 0, 0:4], got.at[c, 1], c, base + 1, xp),
        ]
        for copy in copies:
            copy.start()
        return copies

    def place(target, c, x, y, value):
        target[c, x, y] = value
        if y == 0:
            target[c, x, 4] = from_next(value)

    faces = []

    others = pl.ds(0, (py_size - 1) * per * 16)
    block_waits = [
        pltpu.make_async_remote_copy(
            src_ref=spans.at[c, others], dst_ref=spans.at[c, others],
            send_sem=send_sem.at[5 + c], recv_sem=recv_sem.at[5 + c], device_id=(xn, py), device_id_type=MESH,
        ) for c in range(chunks)
    ]
    halo_wait = pltpu.make_async_remote_copy(
        src_ref=halo, dst_ref=halo, send_sem=send_sem.at[1], recv_sem=recv_sem.at[1],
        device_id=(xn, py), device_id_type=MESH,
    )
    pot_waits = []
    for slot, at in ((0, pl.ds(0, 4)), (2, pl.ds(4, 12))):
        whole = pots.at[0:py_size - 1, at]
        pot_waits.append(pltpu.make_async_remote_copy(
            src_ref=whole, dst_ref=whole, send_sem=send_sem.at[slot], recv_sem=recv_sem.at[slot],
            device_id=(xn, py), device_id_type=MESH,
        ))

    def turn_potential(x):
        flat_pots = pots.reshape(py_size * 16, 128)
        for y0 in range(0, 4, groups):
            loads = []
            for i in range(groups):
                value = (flat_pots[pl.ds(x * 4 + y0 + i, py_size, stride=16), :] - CENTRE) * SCALE
                loads += [value] * per
            pieces = turn_in(loads)
            for i in range(groups):
                diag[x, y0 + i] = pieces[i]

    for c in range(chunks):
        block_waits[c].wait_recv()
        for x in range(4):
            for y0 in range(0, 4, groups):
                pieces = turn_in([
                    states_of(spans.at[c], [s * 16 + x * 4 + y0 + i for s in range(per)], per * 16)
                    for i in range(groups)
                ])
                for i in range(groups):
                    place(v0, c, x, y0 + i, pieces[i])
        if c == 0:
            halo_wait.wait_recv()
        for y0 in range(0, 4, groups):
            pieces = turn_in([
                states_of(halo, [(c * per + s) * 4 + y0 + i for s in range(per)], 8) for i in range(groups)
            ])
            for i in range(groups):
                place(v0, c, 4, y0 + i, pieces[i])
        apply(v0, c1, c)
        if c == 0:
            load_pot.wait()
            pot_waits[0].wait_recv()
            turn_potential(0)
        faces.append(send_faces(c1, v0, r1, c, 0))
    pot_waits[1].wait_recv()
    for x in (1, 2, 3):
        turn_potential(x)
    for c in range(chunks):
        for x in (1, 2, 3):
            for y in range(4):
                place(v1, c, x, y, 0.5 * folded(c1, v0, c, x, y))

    waiting = faces
    faces = []
    for c in range(chunks):
        for copy in waiting[c]:
            copy.wait_recv()
        for x, n in ((0, 0), (4, 1)):
            for y in range(4):
                place(v1, c, x, y, 0.5 * (c1[c, x, y] + r1[c, n, y]))
        apply(v1, c2, c)
        faces.append(send_faces(c2, v1, r2, c, 2))
    for c in range(chunks):
        for x in (1, 2, 3):
            for y in range(4):
                place(v2, c, x, y, folded(c2, v1, c, x, y) - v0[c, x, y])
    sent = waiting + faces

    def edge_copy(c, target):
        return send(
            block_of(send_edge.at[c], target, per * 4), block_of(edge, py * chunks + c, per * 4),
            5 + 2 * chunks + c, xn, target,
        )

    def back_copy(c, target):
        return send(
            block_of(send_back.at[c], target, per * 16), block_of(result, py * chunks + c, per * 16),
            5 + chunks + c, px, target,
        )

    waiting = faces
    for c in range(chunks):
        for copy in waiting[c]:
            copy.wait_recv()
        for x, n in ((0, 0), (4, 1)):
            for y in range(4):
                place(v2, c, x, y, c2[c, x, y] + r2[c, n, y] - v0[c, x, y])
        apply(v2, c3, c)
        for x in range(5):
            for y0 in range(0, 4, groups):
                values = []
                for i in range(groups):
                    value = folded(c3, v2, c, x, y0 + i)
                    if x < 4:
                        value = value - v1[c, x, y0 + i]
                    values.append(value)
                pieces = turn_out(values)
                for i in range(groups):
                    for s in range(per):
                        piece = pieces[i][s * py_size:(s + 1) * py_size]
                        if x < 4:
                            send_back[c, pl.ds(s * 16 + x * 4 + y0 + i, py_size, stride=per * 16), :] = piece
                        else:
                            send_edge[c, pl.ds(s * 4 + y0 + i, py_size, stride=per * 4), :] = piece

        over_all(functools.partial(edge_copy, c))
        over_others(functools.partial(back_copy, c))
        block_of(result, py * chunks + c, per * 16)[...] = block_of(send_back.at[c], py, per * 16)[...]

    edge_waits = [
        pltpu.make_async_remote_copy(
            src_ref=send_edge.at[c], dst_ref=edge.at[0:py_size * per * 4],
            send_sem=send_sem.at[5 + 2 * chunks + c], recv_sem=recv_sem.at[5 + 2 * chunks + c],
            device_id=(xn, py), device_id_type=MESH,
        ) for c in range(chunks)
    ]
    back_waits = [
        pltpu.make_async_remote_copy(
            src_ref=send_back.at[c, others], dst_ref=result.at[others],
            send_sem=send_sem.at[5 + chunks + c], recv_sem=recv_sem.at[5 + chunks + c],
            device_id=(xn, py), device_id_type=MESH,
        ) for c in range(chunks)
    ]
    for wait in edge_waits:
        wait.wait_recv()
    for wait in back_waits:
        wait.wait_recv()
    for s in range(own):
        for y in range(4):
            at = pl.ds(s * 16 + y, py_size, stride=own * 16)
            result[at, :] = result[at, :] + edge[pl.ds(s * 4 + y, py_size, stride=8), :]
    store = pltpu.make_async_copy(result, out_hbm, local_sem.at[0])
    store.start()
    for node in range(16):
        lhs[:, node * 128:(node + 1) * 128] = result[pl.ds(node, STATES, stride=16), :].astype(BF16)
    product = lax.dot_general(lhs[...], block_k[...], (((1,), (1,)), ((), ())), preferred_element_type=F32)
    for n in range(px_size):
        part[n] = product[n * tile_rows:(n + 1) * tile_rows]

    def first_copy(owner):
        return pltpu.make_async_remote_copy(
            src_ref=part.at[owner], dst_ref=got1.at[px], send_sem=send1, recv_sem=recv1,
            device_id=(owner, py), device_id_type=MESH,
        )

    for owner in others_x:
        first_copy(owner).start()
    got1[px] = part[px]
    first_wait = pltpu.make_async_remote_copy(
        src_ref=part.at[0:px_size - 1], dst_ref=got1.at[0:px_size - 1], send_sem=send1, recv_sem=recv1,
        device_id=(xn, py), device_id_type=MESH,
    )
    first_wait.wait_recv()
    total = got1[0]
    for n in range(1, px_size):
        total = total + got1[n]
    sum1[0] = total[:, 0:128]
    sum1[1] = total[:, 128:256]

    def second_copy(target):
        return pltpu.make_async_remote_copy(
            src_ref=sum1.at[target // per_block], dst_ref=got2.at[py], send_sem=send2, recv_sem=recv2,
            device_id=(px, target), device_id_type=MESH,
        )

    over_others(second_copy)
    got2[py] = sum1[py // per_block]
    second_wait = pltpu.make_async_remote_copy(
        src_ref=got2.at[0:py_size - 1], dst_ref=got2.at[0:py_size - 1], send_sem=send2, recv_sem=recv2,
        device_id=(xn, py), device_id_type=MESH,
    )
    second_wait.wait_recv()
    total = got2[0]
    for n in range(1, py_size):
        total = total + got2[n]
    shift = lax.rem(128 - lax.rem(py, per_block) * tile_cols, 128)
    tile_ref[...] = pltpu.roll(total, shift, 1)[:, 0:tile_cols]

    store.wait()
    for wait in block_waits + [halo_wait] + pot_waits + edge_waits + back_waits + [first_wait, second_wait]:
        wait.wait_send()
    for copies in sent:
        for copy in copies:
            copy.wait_send()


def local(px_size, py_size, span, potential, cell_matrix, block):
    chunks = CHUNKS
    own = STATES // py_size
    width = own // chunks * py_size
    rows = width
    field = pltpu.VMEM((chunks, 7, 5, rows, 128), F32)
    faces = pltpu.VMEM((chunks, 2, 4, rows, 128), F32)
    tile = (STATES // px_size, BLOCK // py_size)
    filtered, margin = pl.pallas_call(
        functools.partial(kernel, px_size, py_size, chunks),
        out_shape=(jax.ShapeDtypeStruct((STATES * 16, 128), F32), jax.ShapeDtypeStruct(tile, F32)),
        in_specs=[pl.BlockSpec(memory_space=pltpu.HBM)] * 4,
        out_specs=(pl.BlockSpec(memory_space=pl.ANY), pl.BlockSpec(memory_space=pltpu.VMEM)),
        scratch_shapes=[
            pltpu.VMEM((STATES * 16, 128), F32),
            pltpu.VMEM((125, 125), F32),
            pltpu.VMEM((128, 128), F32),
            pltpu.VMEM((BLOCK * 16, 128), BF16),
            pltpu.VMEM((BLOCK * 16, 128), F32),
            pltpu.VMEM((BLOCK, 2048), BF16),
            pltpu.VMEM((160, 480), BF16),
            pltpu.VMEM((4, 4, rows, 128), F32),
            pltpu.VMEM((chunks, STATES * 16 // chunks, 128), F32),
            pltpu.VMEM((py_size, 16, 128), F32),
            pltpu.VMEM((py_size * 8, 128), F32),
            pltpu.VMEM((py_size * 8, 128), F32),
            field, field, field, field, field, field, faces, faces,
            pltpu.VMEM((chunks, STATES * 16 // chunks, 128), F32),
            pltpu.VMEM((chunks, py_size * 8 // chunks, 128), F32),
            pltpu.VMEM((py_size * 8, 128), F32),
            pltpu.VMEM((STATES * 16, 128), F32),
            pltpu.VMEM((STATES, 2048), BF16),
            pltpu.VMEM((px_size, tile[0], BLOCK), F32),
            pltpu.VMEM((px_size, tile[0], BLOCK), F32),
            pltpu.VMEM((2, tile[0], 128), F32),
            pltpu.VMEM((py_size, tile[0], 128), F32),
            pltpu.SemaphoreType.REGULAR,
            pltpu.SemaphoreType.DMA((4,)),
            pltpu.SemaphoreType.DMA((5 + 3 * chunks,)),
            pltpu.SemaphoreType.DMA((5 + 3 * chunks,)),
            pltpu.SemaphoreType.DMA((chunks, 4)),
            pltpu.SemaphoreType.DMA((chunks, 4)),
            pltpu.SemaphoreType.DMA,
            pltpu.SemaphoreType.DMA,
            pltpu.SemaphoreType.DMA,
            pltpu.SemaphoreType.DMA,
        ],
        compiler_params=pltpu.CompilerParams(
            collective_id=0, has_side_effects=True, vmem_limit_bytes=40 * 1024 * 1024
        ),
    )(*(pltpu.with_memory_space_constraint(value, pltpu.HBM) for value in (
        span.reshape(STATES * 16, 128), potential.reshape(16, 128), cell_matrix, block.reshape(BLOCK * 16, 128)
    )))
    return filtered.reshape(span.shape), margin


def solution(mesh):
    in_specs = (P(None, "px", "py", None), P("px", "py", None), P(), P(None, "px", "py", None))
    out_specs = (P(None, "px", "py", None), P("px", "py"))
    body = functools.partial(local, mesh.shape["px"], mesh.shape["py"])
    return jax.shard_map(body, mesh=mesh, in_specs=in_specs, out_specs=out_specs, check_vma=False)
```

```python
import functools

import jax
import jax.numpy as jnp
from jax import lax
from jax.experimental import pallas as pl
from jax.experimental.pallas import tpu as pltpu
from jax.sharding import PartitionSpec as P

MESH = pl.DeviceIdType.MESH
CENTRE = 13.0
SCALE = 2.0 / 9.0
F32 = jnp.float32
BF16 = jnp.bfloat16
CHUNKS = 2
STATES = 64
BLOCK = 256


def rows_to_lanes(parts, width):
    count = len(parts)
    parts = list(parts)
    group = lax.broadcasted_iota(jnp.int32, parts[0].shape, 1) // width
    bit = count // 2
    while bit:
        low = (group & bit) == 0
        for first in range(count):
            if first & bit:
                continue
            a, b = parts[first], parts[first | bit]
            parts[first] = jnp.where(low, a, pltpu.roll(b, bit * width, 1))
            parts[first | bit] = jnp.where(low, pltpu.roll(a, 128 - bit * width, 1), b)
        bit //= 2
    return parts


def kernel(
    px_size, py_size, chunks,
    span_hbm, pot_hbm, mat_hbm, block_hbm,
    out_hbm, tile_ref,
    span_v, packed, mat_v, mat_pad, block_v, block_f, block_k, mat3, diag,
    spans, pots, halo, face_out,
    v0, v1, v2, c1, c2, c3, r1, r2,
    send_back, send_edge, edge, result, lhs, part, got1, sum1, got2,
    ready, local_sem, send_sem, recv_sem, face_send, face_recv, send1, recv1, send2, recv2,
):
    own = STATES // py_size
    per = own // chunks
    width = per * py_size
    groups = 128 // width
    rows = 128 // groups
    pitch = [per * 16 + 4] + [per * 16] * (chunks - 1)
    px, py = lax.axis_index("px"), lax.axis_index("py")
    xn, xp = lax.rem(px + 1, px_size), lax.rem(px + px_size - 1, px_size)
    tile_rows = STATES // px_size
    tile_cols = BLOCK // py_size

    load_span = pltpu.make_async_copy(span_hbm, span_v, local_sem.at[0])
    load_block = pltpu.make_async_copy(block_hbm, block_v, local_sem.at[1])
    load_mat = pltpu.make_async_copy(mat_hbm, mat_v, local_sem.at[2])
    load_pot = pltpu.make_async_copy(pot_hbm, pots.at[py], local_sem.at[3])
    load_span.start()

    barrier = pltpu.get_barrier_semaphore()

    z_part = [lax.rem(py // 16 + n, 2) * 16 for n in range(2)]
    x_part = [lax.rem(lax.rem(py // 4, 4) + n, 4) * 4 for n in range(4)]
    y_part = [lax.rem(lax.rem(py, 4) + n, 4) for n in range(4)]
    offsets = [(z, x, y) for z in range(2) for x in range(4) for y in range(4)]
    offsets.sort(key=lambda o: (o == (0, 0, 0), -o[0], -(o[0] + min(o[1], 4 - o[1]) + min(o[2], 4 - o[2]))))
    group = [z_part[z] + x_part[x] + y_part[y] for z, x, y in offsets]
    steps = sorted(range(1, px_size), key=lambda n: -min(n, px_size - n))
    others_x = [lax.rem(px + n, px_size) for n in steps]
    plane = lax.rem(py, 16)
    z_own = py // 16
    plane_group = [x_part[x] + y_part[y] for z, x, y in offsets if z == 0][:-1]
    column_group = [(x, lax.rem(z_own + n, 2)) for x in others_x for n in (1, 0)] + [(px, lax.rem(z_own + 1, 2))]

    for x in others_x:
        for y in (py, z_part[1] + plane):
            pl.semaphore_signal(barrier, inc=1, device_id=(x, y), device_id_type=MESH)
    for y in group[:-1]:
        pl.semaphore_signal(barrier, inc=1, device_id=(px, y), device_id_type=MESH)
    mat_pad[...] = jnp.zeros((128, 128), F32)
    part[...] = jnp.zeros(part.shape, F32)
    load_mat.start()
    load_pot.start()
    load_block.start()

    load_span.wait()
    for s in range(own):
        for y in range(4):
            face_out[pl.ds(s * 4 + y, py_size, stride=8), :] = span_v[pl.ds(s * 16 + y, py_size, stride=own * 16), :]

    for r in range(per * 16):
        packed[pl.ds(r, py_size, stride=pitch[0]), :] = span_v[pl.ds(r, py_size, stride=own * 16), :]
    load_pot.wait()
    for y in range(4):
        packed[pl.ds(per * 16 + y, py_size, stride=pitch[0]), :] = jnp.broadcast_to(
            pots[py, y:y + 1, :], (py_size, 128)
        )

    pl.semaphore_wait(barrier, 2 * (px_size - 1) + (py_size - 1))
    for x in (xn, xp):
        pl.semaphore_signal(ready, inc=1, device_id=(x, py), device_id_type=MESH)

    def block_of(ref, index, size):
        return ref.at[pl.ds(pl.multiple_of(index * size, size), size)]

    def send(src, dst, slot, x, y):
        return pltpu.make_async_remote_copy(
            src_ref=src, dst_ref=dst, send_sem=send_sem.at[slot], recv_sem=recv_sem.at[slot],
            device_id=(x, y), device_id_type=MESH,
        )

    def span_copy(c, target):
        if c == 0:
            return send(block_of(packed, target, pitch[0]), block_of(spans.at[0], py, pitch[0]), 5, px, target)
        return send(
            block_of(span_v, target * chunks + c, per * 16), block_of(spans.at[c], py, per * 16), 5 + c, px, target
        )

    def halo_copy(target):
        return send(block_of(face_out, target, 8), block_of(halo, py, 8), 1, xp, target)

    def pot_copy(target):
        at = pl.ds(4, 12)
        return send(pot_hbm.at[at], pots.at[py, at], 2, px, target)

    def over_others(make):
        for target in group[:-1]:
            make(target).start()

    def over_all(make):
        for target in group:
            make(target).start()

    over_others(functools.partial(span_copy, 0))
    pl.semaphore_wait(ready, 2)
    over_all(halo_copy)
    for c in range(1, chunks):
        over_others(functools.partial(span_copy, c))
    spans[0, pl.ds(py * pitch[0], pitch[0]), :] = packed[pl.ds(py * pitch[0], pitch[0]), :]
    for c in range(1, chunks):
        block_of(spans.at[c], py, per * 16)[...] = block_of(span_v, py * chunks + c, per * 16)[...]

    load_mat.wait()
    mat_pad[0:125, 0:125] = mat_v[...]
    scaled = mat_pad[...] * SCALE
    mat_hi = scaled.astype(BF16)
    mat_lo = (scaled - mat_hi.astype(F32)).astype(BF16)
    i = lax.broadcasted_iota(jnp.int32, (160, 128), 0)
    a = lax.broadcasted_iota(jnp.int32, (160, 128), 1)
    pick = jnp.where((i % 32 < 25) & (a == (i % 32) * 5 + i // 32), 1.0, 0.0).astype(BF16)
    j = lax.broadcasted_iota(jnp.int32, (128, 480), 1)
    b = lax.broadcasted_iota(jnp.int32, (128, 480), 0)
    jj = j % 160
    hit = (jj % 32 < 25) & (b == (jj % 32) * 5 + jj // 32)
    middle = (j >= 160) & (j < 320)
    put_hi = jnp.where(hit & jnp.logical_not(middle), 1.0, 0.0).astype(BF16)
    put_lo = jnp.where(hit & middle, 1.0, 0.0).astype(BF16)
    row_hi = jnp.dot(pick, mat_hi, preferred_element_type=F32).astype(BF16)
    row_lo = jnp.dot(pick, mat_lo, preferred_element_type=F32).astype(BF16)
    mat3[...] = (
        jnp.dot(row_hi, put_hi, preferred_element_type=F32) + jnp.dot(row_lo, put_lo, preferred_element_type=F32)
    ).astype(BF16)

    for c in range(chunks):
        for ref in (v0, v1, v2):
            ref[c, 5:7] = jnp.zeros((2, 5, rows, 128), F32)

    load_block.wait()

    def widen(step, carry):
        at = pl.ds(pl.multiple_of(step * 256, 256), 256)
        block_f[at, :] = block_v[at, :].astype(F32)
        return carry

    lax.fori_loop(0, BLOCK * 16 // 256, widen, 0)
    for node in range(16):
        block_k[:, node * 128:(node + 1) * 128] = block_f[pl.ds(node, BLOCK, stride=16), :].astype(BF16)

    over_others(pot_copy)

    lane = lax.broadcasted_iota(jnp.int32, (rows, 128), 1)
    first_cell = lax.rem(lane, py_size) == 0
    last_cell = lax.rem(lane, py_size) == py_size - 1

    def from_next(value):
        return jnp.where(last_cell, pltpu.roll(value, py_size - 1, 1), pltpu.roll(value, 127, 1))

    def from_previous(value):
        return jnp.where(first_cell, pltpu.roll(value, 129 - py_size, 1), pltpu.roll(value, 1, 1))

    def turn_in(loads):
        turned = jnp.concatenate(loads, 0).T
        return rows_to_lanes([turned[h * rows:(h + 1) * rows] for h in range(groups)], width)

    def turn_out(values):
        turned = jnp.concatenate(rows_to_lanes(values, width), 0).T
        return [turned[i * width:(i + 1) * width] for i in range(groups)]

    def states_of(ref, first, pitch):
        loads = [ref[pl.ds(start, py_size, stride=pitch), :] for start in first]
        return jnp.concatenate(loads, 0) if per > 1 else loads[0]

    def flat(ref, c):
        return ref.at[c].reshape(35 * rows, 128)

    def apply(source, contrib, c):
        src, dst = flat(source, c), flat(contrib, c)
        high, low = [], []
        first = None
        for r in range(rows + 1):
            if r < rows:
                value = src[pl.ds(r, 32, stride=rows), :]
                if r == 0:
                    first = value
            else:
                value = pltpu.roll(first, 128 - width, 1)
            h = value.astype(BF16)
            high.append(h)
            low.append((value - h.astype(F32)).astype(BF16))
        carry = None
        first_row = None
        for k in range(0, rows // 4, 2):
            rhs = jnp.concatenate([
                jnp.concatenate(
                    high[4 * n:4 * n + 5] + high[4 * n:4 * n + 5] + low[4 * n:4 * n + 5], 0
                ) for n in (k, k + 1)
            ], 1)
            product = jnp.dot(mat3[...], rhs, preferred_element_type=F32)
            for n in (0, 1):
                mine = product[:, n * 128:(n + 1) * 128]
                for z in range(4):
                    r = 4 * (k + n) + z
                    value = mine[z * 32:(z + 1) * 32]
                    if z == 0 and carry is not None:
                        value = value + carry
                    if r == 0:
                        first_row = value
                    else:
                        dst[pl.ds(r, 32, stride=rows), :] = value
                carry = mine[128:160]
        dst[pl.ds(0, 32, stride=rows), :] = first_row + pltpu.roll(carry, width, 1)

    def folded(contrib, source, c, x, y):
        value = contrib[c, x, y]
        if y == 0:
            value = value + from_previous(contrib[c, x, 4])
        if x < 4:
            value = value + diag[x, y] * source[c, x, y]
        return value

    def face(src, dst, c, slot, x):
        return pltpu.make_async_remote_copy(
            src_ref=src, dst_ref=dst, send_sem=face_send.at[c, slot], recv_sem=face_recv.at[c, slot],
            device_id=(x, py), device_id_type=MESH,
        )

    def send_faces(contrib, source, got, c, base):
        for x in (0, 4):
            for y in range(4):
                contrib[c, x, y] = folded(contrib, source, c, x, y)
        copies = [
            face(contrib.at[c, 4, 0:4], got.at[c, 0], c, base, xn),
            face(contrib.at[c, 0, 0:4], got.at[c, 1], c, base + 1, xp),
        ]
        for copy in copies:
            copy.start()
        return copies

    def place(target, c, x, y, value):
        target[c, x, y] = value
        if y == 0:
            target[c, x, 4] = from_next(value)

    faces = []

    others = pl.ds(0, (py_size - 1) * per * 16)
    block_waits = [
        pltpu.make_async_remote_copy(
            src_ref=spans.at[c, 0:(py_size - 1) * pitch[c]], dst_ref=spans.at[c, 0:(py_size - 1) * pitch[c]],
            send_sem=send_sem.at[5 + c], recv_sem=recv_sem.at[5 + c], device_id=(xn, py), device_id_type=MESH,
        ) for c in range(chunks)
    ]
    halo_wait = pltpu.make_async_remote_copy(
        src_ref=halo, dst_ref=halo, send_sem=send_sem.at[1], recv_sem=recv_sem.at[1],
        device_id=(xn, py), device_id_type=MESH,
    )
    rest = pots.at[0:py_size - 1, 4:16]
    pot_wait = pltpu.make_async_remote_copy(
        src_ref=rest, dst_ref=rest, send_sem=send_sem.at[2], recv_sem=recv_sem.at[2],
        device_id=(xn, py), device_id_type=MESH,
    )

    def turn_potential(x):
        flat_pots = pots.reshape(py_size * 16, 128)
        for y0 in range(0, 4, groups):
            loads = []
            for i in range(groups):
                if x == 0:
                    value = spans[0, pl.ds(per * 16 + y0 + i, py_size, stride=pitch[0]), :]
                else:
                    value = flat_pots[pl.ds(x * 4 + y0 + i, py_size, stride=16), :]
                value = (value - CENTRE) * SCALE
                loads += [value] * per
            pieces = turn_in(loads)
            for i in range(groups):
                diag[x, y0 + i] = pieces[i]

    for c in range(chunks):
        block_waits[c].wait_recv()
        for x in range(4):
            for y0 in range(0, 4, groups):
                pieces = turn_in([
                    states_of(spans.at[c], [s * 16 + x * 4 + y0 + i for s in range(per)], pitch[c])
                    for i in range(groups)
                ])
                for i in range(groups):
                    place(v0, c, x, y0 + i, pieces[i])
        if c == 0:
            halo_wait.wait_recv()
        for y0 in range(0, 4, groups):
            pieces = turn_in([
                states_of(halo, [(c * per + s) * 4 + y0 + i for s in range(per)], 8) for i in range(groups)
            ])
            for i in range(groups):
                place(v0, c, 4, y0 + i, pieces[i])
        apply(v0, c1, c)
        if c == 0:
            turn_potential(0)
        faces.append(send_faces(c1, v0, r1, c, 0))
    pot_wait.wait_recv()
    for x in (1, 2, 3):
        turn_potential(x)
    for c in range(chunks):
        for x in (1, 2, 3):
            for y in range(4):
                place(v1, c, x, y, 0.5 * folded(c1, v0, c, x, y))

    waiting = faces
    faces = []
    for c in range(chunks):
        for copy in waiting[c]:
            copy.wait_recv()
        for x, n in ((0, 0), (4, 1)):
            for y in range(4):
                place(v1, c, x, y, 0.5 * (c1[c, x, y] + r1[c, n, y]))
        apply(v1, c2, c)
        faces.append(send_faces(c2, v1, r2, c, 2))
    for c in range(chunks):
        for x in (1, 2, 3):
            for y in range(4):
                place(v2, c, x, y, folded(c2, v1, c, x, y) - v0[c, x, y])
    sent = waiting + faces

    def edge_copy(c, target):
        return send(
            block_of(send_edge.at[c], target, per * 4), block_of(edge, py * chunks + c, per * 4),
            5 + 2 * chunks + c, xn, target,
        )

    def back_copy(c, target):
        return send(
            block_of(send_back.at[c], target, per * 16), block_of(result, py * chunks + c, per * 16),
            5 + chunks + c, px, target,
        )

    waiting = faces
    for c in range(chunks):
        for copy in waiting[c]:
            copy.wait_recv()
        for x, n in ((0, 0), (4, 1)):
            for y in range(4):
                place(v2, c, x, y, c2[c, x, y] + r2[c, n, y] - v0[c, x, y])
        apply(v2, c3, c)
        for x in range(5):
            for y0 in range(0, 4, groups):
                values = []
                for i in range(groups):
                    value = folded(c3, v2, c, x, y0 + i)
                    if x < 4:
                        value = value - v1[c, x, y0 + i]
                    values.append(value)
                pieces = turn_out(values)
                for i in range(groups):
                    for s in range(per):
                        piece = pieces[i][s * py_size:(s + 1) * py_size]
                        if x < 4:
                            send_back[c, pl.ds(s * 16 + x * 4 + y0 + i, py_size, stride=per * 16), :] = piece
                        else:
                            send_edge[c, pl.ds(s * 4 + y0 + i, py_size, stride=per * 4), :] = piece

        over_all(functools.partial(edge_copy, c))
        over_others(functools.partial(back_copy, c))
        block_of(result, py * chunks + c, per * 16)[...] = block_of(send_back.at[c], py, per * 16)[...]

    edge_waits = [
        pltpu.make_async_remote_copy(
            src_ref=send_edge.at[c], dst_ref=edge.at[0:py_size * per * 4],
            send_sem=send_sem.at[5 + 2 * chunks + c], recv_sem=recv_sem.at[5 + 2 * chunks + c],
            device_id=(xn, py), device_id_type=MESH,
        ) for c in range(chunks)
    ]
    back_waits = [
        pltpu.make_async_remote_copy(
            src_ref=send_back.at[c, others], dst_ref=result.at[others],
            send_sem=send_sem.at[5 + chunks + c], recv_sem=recv_sem.at[5 + chunks + c],
            device_id=(xn, py), device_id_type=MESH,
        ) for c in range(chunks)
    ]
    for wait in edge_waits:
        wait.wait_recv()
    for wait in back_waits:
        wait.wait_recv()
    for s in range(own):
        for y in range(4):
            at = pl.ds(s * 16 + y, py_size, stride=own * 16)
            result[at, :] = result[at, :] + edge[pl.ds(s * 4 + y, py_size, stride=8), :]
    store = pltpu.make_async_copy(result, out_hbm, local_sem.at[0])
    store.start()
    for node in range(16):
        lhs[:, node * 128:(node + 1) * 128] = result[pl.ds(node, STATES, stride=16), :].astype(BF16)
    product = lax.dot_general(block_k[...], lhs[...], (((1,), (1,)), ((), ())), preferred_element_type=F32)
    for n in range(py_size):
        part[n // 16, n % 16, :, 0:STATES] = product[n * tile_cols:(n + 1) * tile_cols]

    def first_copy(target):
        return pltpu.make_async_remote_copy(
            src_ref=part.at[:, target], dst_ref=got1.at[plane], send_sem=send1, recv_sem=recv1,
            device_id=(px, z_part[0] + target), device_id_type=MESH,
        )

    for target in plane_group:
        first_copy(target).start()
    got1[plane] = part[:, plane]
    first_wait = pltpu.make_async_remote_copy(
        src_ref=got1.at[0:15], dst_ref=got1.at[0:15], send_sem=send1, recv_sem=recv1,
        device_id=(xn, py), device_id_type=MESH,
    )
    first_wait.wait_recv()
    total = got1[0]
    for n in range(1, 16):
        total = total + got1[n]
    sum1[...] = total

    def second_copy(x, z):
        return pltpu.make_async_remote_copy(
            src_ref=sum1.at[z], dst_ref=got2.at[px * 2 + z_own], send_sem=send2, recv_sem=recv2,
            device_id=(x, z * 16 + plane), device_id_type=MESH,
        )

    for x, z in column_group:
        second_copy(x, z).start()
    got2[px * 2 + z_own] = sum1[z_own]
    second_wait = pltpu.make_async_remote_copy(
        src_ref=got2.at[0:2 * px_size - 1], dst_ref=got2.at[0:2 * px_size - 1], send_sem=send2, recv_sem=recv2,
        device_id=(xn, py), device_id_type=MESH,
    )
    second_wait.wait_recv()
    total = got2[0]
    for n in range(1, 2 * px_size):
        total = total + got2[n]
    total = pltpu.roll(total, lax.rem(128 - px * tile_rows, 128), 1)
    total = jnp.concatenate([total, jnp.zeros((128 - tile_cols, 128), F32)], 0).T
    tile_ref[...] = total[0:tile_rows, 0:tile_cols]

    store.wait()
    for wait in block_waits + [halo_wait, pot_wait] + edge_waits + back_waits + [first_wait, second_wait]:
        wait.wait_send()
    for copies in sent:
        for copy in copies:
            copy.wait_send()


def local(px_size, py_size, span, potential, cell_matrix, block):
    chunks = CHUNKS
    own = STATES // py_size
    width = own // chunks * py_size
    rows = width
    field = pltpu.VMEM((chunks, 7, 5, rows, 128), F32)
    faces = pltpu.VMEM((chunks, 2, 4, rows, 128), F32)
    tile = (STATES // px_size, BLOCK // py_size)
    filtered, margin = pl.pallas_call(
        functools.partial(kernel, px_size, py_size, chunks),
        out_shape=(jax.ShapeDtypeStruct((STATES * 16, 128), F32), jax.ShapeDtypeStruct(tile, F32)),
        in_specs=[pl.BlockSpec(memory_space=pltpu.HBM)] * 4,
        out_specs=(pl.BlockSpec(memory_space=pl.ANY), pl.BlockSpec(memory_space=pltpu.VMEM)),
        scratch_shapes=[
            pltpu.VMEM((STATES * 16, 128), F32),
            pltpu.VMEM((py_size * (width // py_size * 16 + 4), 128), F32),
            pltpu.VMEM((125, 125), F32),
            pltpu.VMEM((128, 128), F32),
            pltpu.VMEM((BLOCK * 16, 128), BF16),
            pltpu.VMEM((BLOCK * 16, 128), F32),
            pltpu.VMEM((BLOCK, 2048), BF16),
            pltpu.VMEM((160, 480), BF16),
            pltpu.VMEM((4, 4, rows, 128), F32),
            pltpu.VMEM((chunks, py_size * (width // py_size * 16 + 4), 128), F32),
            pltpu.VMEM((py_size, 16, 128), F32),
            pltpu.VMEM((py_size * 8, 128), F32),
            pltpu.VMEM((py_size * 8, 128), F32),
            field, field, field, field, field, field, faces, faces,
            pltpu.VMEM((chunks, STATES * 16 // chunks, 128), F32),
            pltpu.VMEM((chunks, py_size * 8 // chunks, 128), F32),
            pltpu.VMEM((py_size * 8, 128), F32),
            pltpu.VMEM((STATES * 16, 128), F32),
            pltpu.VMEM((STATES, 2048), BF16),
            pltpu.VMEM((2, 16, tile[1], 128), F32),
            pltpu.VMEM((16, 2, tile[1], 128), F32),
            pltpu.VMEM((2, tile[1], 128), F32),
            pltpu.VMEM((2 * px_size, tile[1], 128), F32),
            pltpu.SemaphoreType.REGULAR,
            pltpu.SemaphoreType.DMA((4,)),
            pltpu.SemaphoreType.DMA((5 + 3 * chunks,)),
            pltpu.SemaphoreType.DMA((5 + 3 * chunks,)),
            pltpu.SemaphoreType.DMA((chunks, 4)),
            pltpu.SemaphoreType.DMA((chunks, 4)),
            pltpu.SemaphoreType.DMA,
            pltpu.SemaphoreType.DMA,
            pltpu.SemaphoreType.DMA,
            pltpu.SemaphoreType.DMA,
        ],
        compiler_params=pltpu.CompilerParams(
            collective_id=0, has_side_effects=True, vmem_limit_bytes=40 * 1024 * 1024
        ),
    )(*(pltpu.with_memory_space_constraint(value, pltpu.HBM) for value in (
        span.reshape(STATES * 16, 128), potential.reshape(16, 128), cell_matrix, block.reshape(BLOCK * 16, 128)
    )))
    return filtered.reshape(span.shape), margin


def solution(mesh):
    in_specs = (P(None, "px", "py", None), P("px", "py", None), P(), P(None, "px", "py", None))
    out_specs = (P(None, "px", "py", None), P("px", "py"))
    body = functools.partial(local, mesh.shape["px"], mesh.shape["py"])
    return jax.shard_map(body, mesh=mesh, in_specs=in_specs, out_specs=out_specs, check_vma=False)
```

```python
import functools

import jax
import jax.numpy as jnp
from jax import lax
from jax.experimental import pallas as pl
from jax.experimental.pallas import tpu as pltpu
from jax.sharding import PartitionSpec as P

MESH = pl.DeviceIdType.MESH
CENTRE = 13.0
SCALE = 2.0 / 9.0
F32 = jnp.float32
BF16 = jnp.bfloat16
CHUNKS = 2
STATES = 64
BLOCK = 256


def rows_to_lanes(parts, width):
    count = len(parts)
    parts = list(parts)
    group = lax.broadcasted_iota(jnp.int32, parts[0].shape, 1) // width
    bit = count // 2
    while bit:
        low = (group & bit) == 0
        for first in range(count):
            if first & bit:
                continue
            a, b = parts[first], parts[first | bit]
            parts[first] = jnp.where(low, a, pltpu.roll(b, bit * width, 1))
            parts[first | bit] = jnp.where(low, pltpu.roll(a, 128 - bit * width, 1), b)
        bit //= 2
    return parts


def kernel(
    px_size, py_size, chunks,
    span_hbm, pot_hbm, mat_hbm, block_hbm,
    out_hbm, tile_ref,
    span_v, packed, mat_v, mat_pad, block_v, block_f, block_k, mat3, diag,
    spans, pots, halo, face_out,
    v0, v1, v2, c1, c2, c3, r1, r2,
    send_back, send_edge, edge, result, lhs, part, got1, sum1, got2,
    ready, local_sem, send_sem, recv_sem, face_send, face_recv, send1, recv1, send2, recv2,
):
    own = STATES // py_size
    per = own // chunks
    width = per * py_size
    groups = 128 // width
    rows = 128 // groups
    pitch = [per * 16 + 4] + [per * 16] * (chunks - 1)
    px, py = lax.axis_index("px"), lax.axis_index("py")
    xn, xp = lax.rem(px + 1, px_size), lax.rem(px + px_size - 1, px_size)
    tile_rows = STATES // px_size
    tile_cols = BLOCK // py_size

    load_span = pltpu.make_async_copy(span_hbm, span_v, local_sem.at[0])
    load_block = pltpu.make_async_copy(block_hbm, block_v, local_sem.at[1])
    load_mat = pltpu.make_async_copy(mat_hbm, mat_v, local_sem.at[2])
    load_pot = pltpu.make_async_copy(pot_hbm, pots.at[py], local_sem.at[3])
    load_span.start()

    barrier = pltpu.get_barrier_semaphore()

    z_part = [lax.rem(py // 16 + n, 2) * 16 for n in range(2)]
    x_part = [lax.rem(lax.rem(py // 4, 4) + n, 4) * 4 for n in range(4)]
    y_part = [lax.rem(lax.rem(py, 4) + n, 4) for n in range(4)]
    offsets = [(z, x, y) for z in range(2) for x in range(4) for y in range(4)]
    offsets.sort(key=lambda o: (o == (0, 0, 0), -o[0], -(o[0] + min(o[1], 4 - o[1]) + min(o[2], 4 - o[2]))))
    group = [z_part[z] + x_part[x] + y_part[y] for z, x, y in offsets]
    steps = sorted(range(1, px_size), key=lambda n: -min(n, px_size - n))
    others_x = [lax.rem(px + n, px_size) for n in steps]
    plane = lax.rem(py, 16)
    z_own = py // 16
    plane_group = [x_part[x] + y_part[y] for z, x, y in offsets if z == 0][:-1]
    column_group = [(x, lax.rem(z_own + n, 2)) for x in others_x for n in (1, 0)] + [(px, lax.rem(z_own + 1, 2))]

    for x in others_x:
        for y in (py, z_part[1] + plane):
            pl.semaphore_signal(barrier, inc=1, device_id=(x, y), device_id_type=MESH)
    for y in group[:-1]:
        pl.semaphore_signal(barrier, inc=1, device_id=(px, y), device_id_type=MESH)
    mat_pad[...] = jnp.zeros((128, 128), F32)
    part[...] = jnp.zeros(part.shape, F32)
    load_mat.start()
    load_pot.start()
    load_block.start()

    load_span.wait()
    for s in range(own):
        for y in range(4):
            face_out[pl.ds(s * 4 + y, py_size, stride=8), :] = span_v[pl.ds(s * 16 + y, py_size, stride=own * 16), :]

    for r in range(per * 16):
        packed[pl.ds(r, py_size, stride=pitch[0]), :] = span_v[pl.ds(r, py_size, stride=own * 16), :]
    load_pot.wait()
    for y in range(4):
        packed[pl.ds(per * 16 + y, py_size, stride=pitch[0]), :] = jnp.broadcast_to(
            pots[py, y:y + 1, :], (py_size, 128)
        )

    pl.semaphore_wait(barrier, 2 * (px_size - 1) + (py_size - 1))
    for x in (xn, xp):
        pl.semaphore_signal(ready, inc=1, device_id=(x, py), device_id_type=MESH)

    def block_of(ref, index, size):
        return ref.at[pl.ds(pl.multiple_of(index * size, size), size)]

    def send(src, dst, slot, x, y):
        return pltpu.make_async_remote_copy(
            src_ref=src, dst_ref=dst, send_sem=send_sem.at[slot], recv_sem=recv_sem.at[slot],
            device_id=(x, y), device_id_type=MESH,
        )

    def span_copy(c, target):
        if c == 0:
            return send(block_of(packed, target, pitch[0]), block_of(spans.at[0], py, pitch[0]), 5, px, target)
        return send(
            block_of(span_v, target * chunks + c, per * 16), block_of(spans.at[c], py, per * 16), 5 + c, px, target
        )

    def halo_copy(target):
        return send(block_of(face_out, target, 8), block_of(halo, py, 8), 1, xp, target)

    def pot_copy(target):
        at = pl.ds(4, 12)
        return send(pot_hbm.at[at], pots.at[py, at], 2, px, target)

    def over_others(make):
        for target in group[:-1]:
            make(target).start()

    def over_all(make):
        for target in group:
            make(target).start()

    for target in group[:16]:
        span_copy(0, target).start()
    pl.semaphore_wait(ready, 2)
    over_all(halo_copy)
    for target in group[16:-1]:
        span_copy(0, target).start()
    for c in range(1, chunks):
        over_others(functools.partial(span_copy, c))
    spans[0, pl.ds(py * pitch[0], pitch[0]), :] = packed[pl.ds(py * pitch[0], pitch[0]), :]
    for c in range(1, chunks):
        block_of(spans.at[c], py, per * 16)[...] = block_of(span_v, py * chunks + c, per * 16)[...]

    load_mat.wait()
    mat_pad[0:125, 0:125] = mat_v[...]
    scaled = mat_pad[...] * SCALE
    mat_hi = scaled.astype(BF16)
    mat_lo = (scaled - mat_hi.astype(F32)).astype(BF16)
    i = lax.broadcasted_iota(jnp.int32, (160, 128), 0)
    a = lax.broadcasted_iota(jnp.int32, (160, 128), 1)
    pick = jnp.where((i % 32 < 25) & (a == (i % 32) * 5 + i // 32), 1.0, 0.0).astype(BF16)
    j = lax.broadcasted_iota(jnp.int32, (128, 480), 1)
    b = lax.broadcasted_iota(jnp.int32, (128, 480), 0)
    jj = j % 160
    hit = (jj % 32 < 25) & (b == (jj % 32) * 5 + jj // 32)
    middle = (j >= 160) & (j < 320)
    put_hi = jnp.where(hit & jnp.logical_not(middle), 1.0, 0.0).astype(BF16)
    put_lo = jnp.where(hit & middle, 1.0, 0.0).astype(BF16)
    row_hi = jnp.dot(pick, mat_hi, preferred_element_type=F32).astype(BF16)
    row_lo = jnp.dot(pick, mat_lo, preferred_element_type=F32).astype(BF16)
    mat3[...] = (
        jnp.dot(row_hi, put_hi, preferred_element_type=F32) + jnp.dot(row_lo, put_lo, preferred_element_type=F32)
    ).astype(BF16)

    for c in range(chunks):
        for ref in (v0, v1, v2):
            ref[c, 5:7] = jnp.zeros((2, 5, rows, 128), F32)

    load_block.wait()

    def widen(step, carry):
        at = pl.ds(pl.multiple_of(step * 256, 256), 256)
        block_f[at, :] = block_v[at, :].astype(F32)
        return carry

    lax.fori_loop(0, BLOCK * 16 // 256, widen, 0)
    for node in range(16):
        block_k[:, node * 128:(node + 1) * 128] = block_f[pl.ds(node, BLOCK, stride=16), :].astype(BF16)


    lane = lax.broadcasted_iota(jnp.int32, (rows, 128), 1)
    first_cell = lax.rem(lane, py_size) == 0
    last_cell = lax.rem(lane, py_size) == py_size - 1

    def from_next(value):
        return jnp.where(last_cell, pltpu.roll(value, py_size - 1, 1), pltpu.roll(value, 127, 1))

    def from_previous(value):
        return jnp.where(first_cell, pltpu.roll(value, 129 - py_size, 1), pltpu.roll(value, 1, 1))

    def turn_in(loads):
        turned = jnp.concatenate(loads, 0).T
        return rows_to_lanes([turned[h * rows:(h + 1) * rows] for h in range(groups)], width)

    def turn_out(values):
        turned = jnp.concatenate(rows_to_lanes(values, width), 0).T
        return [turned[i * width:(i + 1) * width] for i in range(groups)]

    def states_of(ref, first, pitch):
        loads = [ref[pl.ds(start, py_size, stride=pitch), :] for start in first]
        return jnp.concatenate(loads, 0) if per > 1 else loads[0]

    def flat(ref, c):
        return ref.at[c].reshape(35 * rows, 128)

    def apply(source, contrib, c):
        src, dst = flat(source, c), flat(contrib, c)
        high, low = [], []
        first = None
        for r in range(rows + 1):
            if r < rows:
                value = src[pl.ds(r, 32, stride=rows), :]
                if r == 0:
                    first = value
            else:
                value = pltpu.roll(first, 128 - width, 1)
            h = value.astype(BF16)
            high.append(h)
            low.append((value - h.astype(F32)).astype(BF16))
        carry = None
        first_row = None
        for k in range(0, rows // 4, 2):
            rhs = jnp.concatenate([
                jnp.concatenate(
                    high[4 * n:4 * n + 5] + high[4 * n:4 * n + 5] + low[4 * n:4 * n + 5], 0
                ) for n in (k, k + 1)
            ], 1)
            product = jnp.dot(mat3[...], rhs, preferred_element_type=F32)
            for n in (0, 1):
                mine = product[:, n * 128:(n + 1) * 128]
                for z in range(4):
                    r = 4 * (k + n) + z
                    value = mine[z * 32:(z + 1) * 32]
                    if z == 0 and carry is not None:
                        value = value + carry
                    if r == 0:
                        first_row = value
                    else:
                        dst[pl.ds(r, 32, stride=rows), :] = value
                carry = mine[128:160]
        dst[pl.ds(0, 32, stride=rows), :] = first_row + pltpu.roll(carry, width, 1)

    def folded(contrib, source, c, x, y):
        value = contrib[c, x, y]
        if y == 0:
            value = value + from_previous(contrib[c, x, 4])
        if x < 4:
            value = value + diag[x, y] * source[c, x, y]
        return value

    def face(src, dst, c, slot, x):
        return pltpu.make_async_remote_copy(
            src_ref=src, dst_ref=dst, send_sem=face_send.at[c, slot], recv_sem=face_recv.at[c, slot],
            device_id=(x, py), device_id_type=MESH,
        )

    def send_faces(contrib, source, got, c, base):
        for x in (0, 4):
            for y in range(4):
                contrib[c, x, y] = folded(contrib, source, c, x, y)
        copies = [
            face(contrib.at[c, 4, 0:4], got.at[c, 0], c, base, xn),
            face(contrib.at[c, 0, 0:4], got.at[c, 1], c, base + 1, xp),
        ]
        for copy in copies:
            copy.start()
        return copies

    def place(target, c, x, y, value):
        target[c, x, y] = value
        if y == 0:
            target[c, x, 4] = from_next(value)

    faces = []

    others = pl.ds(0, (py_size - 1) * per * 16)
    block_waits = [
        pltpu.make_async_remote_copy(
            src_ref=spans.at[c, 0:(py_size - 1) * pitch[c]], dst_ref=spans.at[c, 0:(py_size - 1) * pitch[c]],
            send_sem=send_sem.at[5 + c], recv_sem=recv_sem.at[5 + c], device_id=(xn, py), device_id_type=MESH,
        ) for c in range(chunks)
    ]
    halo_wait = pltpu.make_async_remote_copy(
        src_ref=halo, dst_ref=halo, send_sem=send_sem.at[1], recv_sem=recv_sem.at[1],
        device_id=(xn, py), device_id_type=MESH,
    )
    rest = pots.at[0:py_size - 1, 4:16]
    pot_wait = pltpu.make_async_remote_copy(
        src_ref=rest, dst_ref=rest, send_sem=send_sem.at[2], recv_sem=recv_sem.at[2],
        device_id=(xn, py), device_id_type=MESH,
    )

    def turn_potential(x):
        flat_pots = pots.reshape(py_size * 16, 128)
        for y0 in range(0, 4, groups):
            loads = []
            for i in range(groups):
                if x == 0:
                    value = spans[0, pl.ds(per * 16 + y0 + i, py_size, stride=pitch[0]), :]
                else:
                    value = flat_pots[pl.ds(x * 4 + y0 + i, py_size, stride=16), :]
                value = (value - CENTRE) * SCALE
                loads += [value] * per
            pieces = turn_in(loads)
            for i in range(groups):
                diag[x, y0 + i] = pieces[i]

    for c in range(chunks):
        block_waits[c].wait_recv()
        if c == 0:
            over_others(pot_copy)
        for x in range(4):
            for y0 in range(0, 4, groups):
                pieces = turn_in([
                    states_of(spans.at[c], [s * 16 + x * 4 + y0 + i for s in range(per)], pitch[c])
                    for i in range(groups)
                ])
                for i in range(groups):
                    place(v0, c, x, y0 + i, pieces[i])
        if c == 0:
            halo_wait.wait_recv()
        for y0 in range(0, 4, groups):
            pieces = turn_in([
                states_of(halo, [(c * per + s) * 4 + y0 + i for s in range(per)], 8) for i in range(groups)
            ])
            for i in range(groups):
                place(v0, c, 4, y0 + i, pieces[i])
        apply(v0, c1, c)
        if c == 0:
            turn_potential(0)
        faces.append(send_faces(c1, v0, r1, c, 0))
    pot_wait.wait_recv()
    for x in (1, 2, 3):
        turn_potential(x)
    for c in range(chunks):
        for x in (1, 2, 3):
            for y in range(4):
                place(v1, c, x, y, 0.5 * folded(c1, v0, c, x, y))

    waiting = faces
    faces = []
    for c in range(chunks):
        for copy in waiting[c]:
            copy.wait_recv()
        for x, n in ((0, 0), (4, 1)):
            for y in range(4):
                place(v1, c, x, y, 0.5 * (c1[c, x, y] + r1[c, n, y]))
        apply(v1, c2, c)
        faces.append(send_faces(c2, v1, r2, c, 2))
    for c in range(chunks):
        for x in (1, 2, 3):
            for y in range(4):
                place(v2, c, x, y, folded(c2, v1, c, x, y) - v0[c, x, y])
    sent = waiting + faces

    def edge_copy(c, target):
        return send(
            block_of(send_edge.at[c], target, per * 4), block_of(edge, py * chunks + c, per * 4),
            5 + 2 * chunks + c, xn, target,
        )

    def back_copy(c, target):
        return send(
            block_of(send_back.at[c], target, per * 16), block_of(result, py * chunks + c, per * 16),
            5 + chunks + c, px, target,
        )

    waiting = faces
    for c in range(chunks):
        for copy in waiting[c]:
            copy.wait_recv()
        for x, n in ((0, 0), (4, 1)):
            for y in range(4):
                place(v2, c, x, y, c2[c, x, y] + r2[c, n, y] - v0[c, x, y])
        apply(v2, c3, c)
        for x in range(5):
            for y0 in range(0, 4, groups):
                values = []
                for i in range(groups):
                    value = folded(c3, v2, c, x, y0 + i)
                    if x < 4:
                        value = value - v1[c, x, y0 + i]
                    values.append(value)
                pieces = turn_out(values)
                for i in range(groups):
                    for s in range(per):
                        piece = pieces[i][s * py_size:(s + 1) * py_size]
                        if x < 4:
                            send_back[c, pl.ds(s * 16 + x * 4 + y0 + i, py_size, stride=per * 16), :] = piece
                        else:
                            send_edge[c, pl.ds(s * 4 + y0 + i, py_size, stride=per * 4), :] = piece

        over_all(functools.partial(edge_copy, c))
        over_others(functools.partial(back_copy, c))
        block_of(result, py * chunks + c, per * 16)[...] = block_of(send_back.at[c], py, per * 16)[...]

    edge_waits = [
        pltpu.make_async_remote_copy(
            src_ref=send_edge.at[c], dst_ref=edge.at[0:py_size * per * 4],
            send_sem=send_sem.at[5 + 2 * chunks + c], recv_sem=recv_sem.at[5 + 2 * chunks + c],
            device_id=(xn, py), device_id_type=MESH,
        ) for c in range(chunks)
    ]
    back_waits = [
        pltpu.make_async_remote_copy(
            src_ref=send_back.at[c, others], dst_ref=result.at[others],
            send_sem=send_sem.at[5 + chunks + c], recv_sem=recv_sem.at[5 + chunks + c],
            device_id=(xn, py), device_id_type=MESH,
        ) for c in range(chunks)
    ]
    for wait in edge_waits:
        wait.wait_recv()
    for wait in back_waits:
        wait.wait_recv()
    for s in range(own):
        for y in range(4):
            at = pl.ds(s * 16 + y, py_size, stride=own * 16)
            result[at, :] = result[at, :] + edge[pl.ds(s * 4 + y, py_size, stride=8), :]
    store = pltpu.make_async_copy(result, out_hbm, local_sem.at[0])
    store.start()
    for node in range(16):
        lhs[:, node * 128:(node + 1) * 128] = result[pl.ds(node, STATES, stride=16), :].astype(BF16)
    product = lax.dot_general(block_k[...], lhs[...], (((1,), (1,)), ((), ())), preferred_element_type=F32)
    for n in range(py_size):
        part[n // 16, n % 16, :, 0:STATES] = product[n * tile_cols:(n + 1) * tile_cols]

    def first_copy(target):
        return pltpu.make_async_remote_copy(
            src_ref=part.at[:, target], dst_ref=got1.at[plane], send_sem=send1, recv_sem=recv1,
            device_id=(px, z_part[0] + target), device_id_type=MESH,
        )

    for target in plane_group:
        first_copy(target).start()
    got1[plane] = part[:, plane]
    first_wait = pltpu.make_async_remote_copy(
        src_ref=got1.at[0:15], dst_ref=got1.at[0:15], send_sem=send1, recv_sem=recv1,
        device_id=(xn, py), device_id_type=MESH,
    )
    first_wait.wait_recv()
    total = got1[0]
    for n in range(1, 16):
        total = total + got1[n]
    sum1[...] = total

    def second_copy(x, z):
        return pltpu.make_async_remote_copy(
            src_ref=sum1.at[z], dst_ref=got2.at[px * 2 + z_own], send_sem=send2, recv_sem=recv2,
            device_id=(x, z * 16 + plane), device_id_type=MESH,
        )

    for x, z in column_group:
        second_copy(x, z).start()
    got2[px * 2 + z_own] = sum1[z_own]
    second_wait = pltpu.make_async_remote_copy(
        src_ref=got2.at[0:2 * px_size - 1], dst_ref=got2.at[0:2 * px_size - 1], send_sem=send2, recv_sem=recv2,
        device_id=(xn, py), device_id_type=MESH,
    )
    second_wait.wait_recv()
    total = got2[0]
    for n in range(1, 2 * px_size):
        total = total + got2[n]
    total = pltpu.roll(total, lax.rem(128 - px * tile_rows, 128), 1)
    total = jnp.concatenate([total, jnp.zeros((128 - tile_cols, 128), F32)], 0).T
    tile_ref[...] = total[0:tile_rows, 0:tile_cols]

    store.wait()
    for wait in block_waits + [halo_wait, pot_wait] + edge_waits + back_waits + [first_wait, second_wait]:
        wait.wait_send()
    for copies in sent:
        for copy in copies:
            copy.wait_send()


def local(px_size, py_size, span, potential, cell_matrix, block):
    chunks = CHUNKS
    own = STATES // py_size
    width = own // chunks * py_size
    rows = width
    field = pltpu.VMEM((chunks, 7, 5, rows, 128), F32)
    faces = pltpu.VMEM((chunks, 2, 4, rows, 128), F32)
    tile = (STATES // px_size, BLOCK // py_size)
    filtered, margin = pl.pallas_call(
        functools.partial(kernel, px_size, py_size, chunks),
        out_shape=(jax.ShapeDtypeStruct((STATES * 16, 128), F32), jax.ShapeDtypeStruct(tile, F32)),
        in_specs=[pl.BlockSpec(memory_space=pltpu.HBM)] * 4,
        out_specs=(pl.BlockSpec(memory_space=pl.ANY), pl.BlockSpec(memory_space=pltpu.VMEM)),
        scratch_shapes=[
            pltpu.VMEM((STATES * 16, 128), F32),
            pltpu.VMEM((py_size * (width // py_size * 16 + 4), 128), F32),
            pltpu.VMEM((125, 125), F32),
            pltpu.VMEM((128, 128), F32),
            pltpu.VMEM((BLOCK * 16, 128), BF16),
            pltpu.VMEM((BLOCK * 16, 128), F32),
            pltpu.VMEM((BLOCK, 2048), BF16),
            pltpu.VMEM((160, 480), BF16),
            pltpu.VMEM((4, 4, rows, 128), F32),
            pltpu.VMEM((chunks, py_size * (width // py_size * 16 + 4), 128), F32),
            pltpu.VMEM((py_size, 16, 128), F32),
            pltpu.VMEM((py_size * 8, 128), F32),
            pltpu.VMEM((py_size * 8, 128), F32),
            field, field, field, field, field, field, faces, faces,
            pltpu.VMEM((chunks, STATES * 16 // chunks, 128), F32),
            pltpu.VMEM((chunks, py_size * 8 // chunks, 128), F32),
            pltpu.VMEM((py_size * 8, 128), F32),
            pltpu.VMEM((STATES * 16, 128), F32),
            pltpu.VMEM((STATES, 2048), BF16),
            pltpu.VMEM((2, 16, tile[1], 128), F32),
            pltpu.VMEM((16, 2, tile[1], 128), F32),
            pltpu.VMEM((2, tile[1], 128), F32),
            pltpu.VMEM((2 * px_size, tile[1], 128), F32),
            pltpu.SemaphoreType.REGULAR,
            pltpu.SemaphoreType.DMA((4,)),
            pltpu.SemaphoreType.DMA((5 + 3 * chunks,)),
            pltpu.SemaphoreType.DMA((5 + 3 * chunks,)),
            pltpu.SemaphoreType.DMA((chunks, 4)),
            pltpu.SemaphoreType.DMA((chunks, 4)),
            pltpu.SemaphoreType.DMA,
            pltpu.SemaphoreType.DMA,
            pltpu.SemaphoreType.DMA,
            pltpu.SemaphoreType.DMA,
        ],
        compiler_params=pltpu.CompilerParams(
            collective_id=0, has_side_effects=True, vmem_limit_bytes=40 * 1024 * 1024
        ),
    )(*(pltpu.with_memory_space_constraint(value, pltpu.HBM) for value in (
        span.reshape(STATES * 16, 128), potential.reshape(16, 128), cell_matrix, block.reshape(BLOCK * 16, 128)
    )))
    return filtered.reshape(span.shape), margin


def solution(mesh):
    in_specs = (P(None, "px", "py", None), P("px", "py", None), P(), P(None, "px", "py", None))
    out_specs = (P(None, "px", "py", None), P("px", "py"))
    body = functools.partial(local, mesh.shape["px"], mesh.shape["py"])
    return jax.shard_map(body, mesh=mesh, in_specs=in_specs, out_specs=out_specs, check_vma=False)
```

```python
import functools

import jax
import jax.numpy as jnp
from jax import lax
from jax.experimental import pallas as pl
from jax.experimental.pallas import tpu as pltpu
from jax.sharding import PartitionSpec as P

MESH = pl.DeviceIdType.MESH
CENTRE = 13.0
SCALE = 2.0 / 9.0
F32 = jnp.float32
BF16 = jnp.bfloat16
CHUNKS = 2
STATES = 64
BLOCK = 256


def rows_to_lanes(parts, width):
    count = len(parts)
    parts = list(parts)
    group = lax.broadcasted_iota(jnp.int32, parts[0].shape, 1) // width
    bit = count // 2
    while bit:
        low = (group & bit) == 0
        for first in range(count):
            if first & bit:
                continue
            a, b = parts[first], parts[first | bit]
            parts[first] = jnp.where(low, a, pltpu.roll(b, bit * width, 1))
            parts[first | bit] = jnp.where(low, pltpu.roll(a, 128 - bit * width, 1), b)
        bit //= 2
    return parts


def kernel(
    px_size, py_size, chunks,
    span_hbm, pot_hbm, mat_hbm, block_hbm,
    out_hbm, tile_ref,
    span_v, packed, mat_v, mat_pad, block_v, block_f, block_k, mat3, diag,
    spans, pots, halo, face_out,
    v0, v1, v2, c1, c2, c3, r1, r2,
    send_back, send_edge, edge, result, lhs, part, got1, sum1, got2,
    ready, local_sem, send_sem, recv_sem, face_send, face_recv, send1, recv1, send2, recv2,
):
    own = STATES // py_size
    per = own // chunks
    width = per * py_size
    groups = 128 // width
    rows = 128 // groups
    pitch = [per * 16 + 4] + [per * 16] * (chunks - 1)
    px, py = lax.axis_index("px"), lax.axis_index("py")
    xn, xp = lax.rem(px + 1, px_size), lax.rem(px + px_size - 1, px_size)
    tile_rows = STATES // px_size
    tile_cols = BLOCK // py_size

    load_span = pltpu.make_async_copy(span_hbm, span_v, local_sem.at[0])
    load_block = pltpu.make_async_copy(block_hbm, block_v, local_sem.at[1])
    load_mat = pltpu.make_async_copy(mat_hbm, mat_v, local_sem.at[2])
    load_pot = pltpu.make_async_copy(pot_hbm, pots.at[py], local_sem.at[3])
    load_span.start()

    barrier = pltpu.get_barrier_semaphore()

    z_part = [lax.rem(py // 16 + n, 2) * 16 for n in range(2)]
    x_part = [lax.rem(lax.rem(py // 4, 4) + n, 4) * 4 for n in range(4)]
    y_part = [lax.rem(lax.rem(py, 4) + n, 4) for n in range(4)]
    offsets = [(z, x, y) for z in range(2) for x in range(4) for y in range(4)]
    offsets.sort(key=lambda o: (o == (0, 0, 0), -o[0], -(o[0] + min(o[1], 4 - o[1]) + min(o[2], 4 - o[2]))))
    group = [z_part[z] + x_part[x] + y_part[y] for z, x, y in offsets]
    steps = sorted(range(1, px_size), key=lambda n: -min(n, px_size - n))
    others_x = [lax.rem(px + n, px_size) for n in steps]
    plane = lax.rem(py, 16)
    z_own = py // 16
    plane_group = [x_part[x] + y_part[y] for z, x, y in offsets if z == 0][:-1]
    column_group = [(x, lax.rem(z_own + n, 2)) for x in others_x for n in (1, 0)] + [(px, lax.rem(z_own + 1, 2))]

    for x in others_x:
        for y in (py, z_part[1] + plane):
            pl.semaphore_signal(barrier, inc=1, device_id=(x, y), device_id_type=MESH)
    for y in group[:-1]:
        pl.semaphore_signal(barrier, inc=1, device_id=(px, y), device_id_type=MESH)
    mat_pad[...] = jnp.zeros((128, 128), F32)
    part[...] = jnp.zeros(part.shape, F32)
    load_mat.start()
    load_pot.start()
    load_block.start()

    load_span.wait()
    for s in range(own):
        for y in range(4):
            face_out[pl.ds(s * 4 + y, py_size, stride=8), :] = span_v[pl.ds(s * 16 + y, py_size, stride=own * 16), :]

    for r in range(per * 16):
        packed[pl.ds(r, py_size, stride=pitch[0]), :] = span_v[pl.ds(r, py_size, stride=own * 16), :]
    load_pot.wait()
    for y in range(4):
        packed[pl.ds(per * 16 + y, py_size, stride=pitch[0]), :] = jnp.broadcast_to(
            pots[py, y:y + 1, :], (py_size, 128)
        )

    pl.semaphore_wait(barrier, 2 * (px_size - 1) + (py_size - 1))
    for x in (xn, xp):
        pl.semaphore_signal(ready, inc=1, device_id=(x, py), device_id_type=MESH)

    def block_of(ref, index, size):
        return ref.at[pl.ds(pl.multiple_of(index * size, size), size)]

    def send(src, dst, slot, x, y):
        return pltpu.make_async_remote_copy(
            src_ref=src, dst_ref=dst, send_sem=send_sem.at[slot], recv_sem=recv_sem.at[slot],
            device_id=(x, y), device_id_type=MESH,
        )

    def span_copy(c, target):
        if c == 0:
            return send(block_of(packed, target, pitch[0]), block_of(spans.at[0], py, pitch[0]), 5, px, target)
        return send(
            block_of(span_v, target * chunks + c, per * 16), block_of(spans.at[c], py, per * 16), 5 + c, px, target
        )

    def halo_copy(target):
        return send(block_of(face_out, target, 8), block_of(halo, py, 8), 1, xp, target)

    def pot_copy(target):
        at = pl.ds(4, 12)
        return send(pot_hbm.at[at], pots.at[py, at], 2, px, target)

    def over_others(make):
        for target in group[:-1]:
            make(target).start()

    def over_all(make):
        for target in group:
            make(target).start()

    for target in group[:16]:
        span_copy(0, target).start()
    pl.semaphore_wait(ready, 2)
    over_all(halo_copy)
    for target in group[16:-1]:
        span_copy(0, target).start()
    for c in range(1, chunks):
        over_others(functools.partial(span_copy, c))
    spans[0, pl.ds(py * pitch[0], pitch[0]), :] = packed[pl.ds(py * pitch[0], pitch[0]), :]
    for c in range(1, chunks):
        block_of(spans.at[c], py, per * 16)[...] = block_of(span_v, py * chunks + c, per * 16)[...]

    load_mat.wait()
    mat_pad[0:125, 0:125] = mat_v[...]
    scaled = mat_pad[...] * SCALE
    mat_hi = scaled.astype(BF16)
    mat_lo = (scaled - mat_hi.astype(F32)).astype(BF16)
    i = lax.broadcasted_iota(jnp.int32, (160, 128), 0)
    a = lax.broadcasted_iota(jnp.int32, (160, 128), 1)
    pick = jnp.where((i % 32 < 25) & (a == (i % 32) * 5 + i // 32), 1.0, 0.0).astype(BF16)
    j = lax.broadcasted_iota(jnp.int32, (128, 480), 1)
    b = lax.broadcasted_iota(jnp.int32, (128, 480), 0)
    jj = j % 160
    hit = (jj % 32 < 25) & (b == (jj % 32) * 5 + jj // 32)
    middle = (j >= 160) & (j < 320)
    put_hi = jnp.where(hit & jnp.logical_not(middle), 1.0, 0.0).astype(BF16)
    put_lo = jnp.where(hit & middle, 1.0, 0.0).astype(BF16)
    row_hi = jnp.dot(pick, mat_hi, preferred_element_type=F32).astype(BF16)
    row_lo = jnp.dot(pick, mat_lo, preferred_element_type=F32).astype(BF16)
    mat3[...] = (
        jnp.dot(row_hi, put_hi, preferred_element_type=F32) + jnp.dot(row_lo, put_lo, preferred_element_type=F32)
    ).astype(BF16)

    for c in range(chunks):
        for ref in (v0, v1, v2):
            ref[c, 5:7] = jnp.zeros((2, 5, rows, 128), F32)

    load_block.wait()

    def widen(step, carry):
        at = pl.ds(pl.multiple_of(step * 256, 256), 256)
        block_f[at, :] = block_v[at, :].astype(F32)
        return carry

    lax.fori_loop(0, BLOCK * 16 // 256, widen, 0)
    for node in range(16):
        block_k[:, node * 128:(node + 1) * 128] = block_f[pl.ds(node, BLOCK, stride=16), :].astype(BF16)

    over_others(pot_copy)

    lane = lax.broadcasted_iota(jnp.int32, (rows, 128), 1)
    first_cell = lax.rem(lane, py_size) == 0
    last_cell = lax.rem(lane, py_size) == py_size - 1

    def from_next(value):
        return jnp.where(last_cell, pltpu.roll(value, py_size - 1, 1), pltpu.roll(value, 127, 1))

    def from_previous(value):
        return jnp.where(first_cell, pltpu.roll(value, 129 - py_size, 1), pltpu.roll(value, 1, 1))

    def turn_in(loads):
        turned = jnp.concatenate(loads, 0).T
        return rows_to_lanes([turned[h * rows:(h + 1) * rows] for h in range(groups)], width)

    def turn_out(values):
        turned = jnp.concatenate(rows_to_lanes(values, width), 0).T
        return [turned[i * width:(i + 1) * width] for i in range(groups)]

    def states_of(ref, first, pitch):
        loads = [ref[pl.ds(start, py_size, stride=pitch), :] for start in first]
        return jnp.concatenate(loads, 0) if per > 1 else loads[0]

    def flat(ref, c):
        return ref.at[c].reshape(35 * rows, 128)

    def apply(source, contrib, c):
        src, dst = flat(source, c), flat(contrib, c)
        high, low = [], []
        first = None
        for r in range(rows + 1):
            if r < rows:
                value = src[pl.ds(r, 32, stride=rows), :]
                if r == 0:
                    first = value
            else:
                value = pltpu.roll(first, 128 - width, 1)
            h = value.astype(BF16)
            high.append(h)
            low.append((value - h.astype(F32)).astype(BF16))
        carry = None
        first_row = None
        for k in range(0, rows // 4, 2):
            rhs = jnp.concatenate([
                jnp.concatenate(
                    high[4 * n:4 * n + 5] + high[4 * n:4 * n + 5] + low[4 * n:4 * n + 5], 0
                ) for n in (k, k + 1)
            ], 1)
            product = jnp.dot(mat3[...], rhs, preferred_element_type=F32)
            for n in (0, 1):
                mine = product[:, n * 128:(n + 1) * 128]
                for z in range(4):
                    r = 4 * (k + n) + z
                    value = mine[z * 32:(z + 1) * 32]
                    if z == 0 and carry is not None:
                        value = value + carry
                    if r == 0:
                        first_row = value
                    else:
                        dst[pl.ds(r, 32, stride=rows), :] = value
                carry = mine[128:160]
        dst[pl.ds(0, 32, stride=rows), :] = first_row + pltpu.roll(carry, width, 1)

    def folded(contrib, source, c, x, y):
        value = contrib[c, x, y]
        if y == 0:
            value = value + from_previous(contrib[c, x, 4])
        if x < 4:
            value = value + diag[x, y] * source[c, x, y]
        return value

    def face(src, dst, c, slot, x):
        return pltpu.make_async_remote_copy(
            src_ref=src, dst_ref=dst, send_sem=face_send.at[c, slot], recv_sem=face_recv.at[c, slot],
            device_id=(x, py), device_id_type=MESH,
        )

    def send_faces(contrib, source, got, c, base):
        for x in (0, 4):
            for y in range(4):
                contrib[c, x, y] = folded(contrib, source, c, x, y)
        copies = [
            face(contrib.at[c, 4, 0:4], got.at[c, 0], c, base, xn),
            face(contrib.at[c, 0, 0:4], got.at[c, 1], c, base + 1, xp),
        ]
        for copy in copies:
            copy.start()
        return copies

    def place(target, c, x, y, value):
        target[c, x, y] = value
        if y == 0:
            target[c, x, 4] = from_next(value)

    faces = []

    others = pl.ds(0, (py_size - 1) * per * 16)
    block_waits = [
        pltpu.make_async_remote_copy(
            src_ref=spans.at[c, 0:(py_size - 1) * pitch[c]], dst_ref=spans.at[c, 0:(py_size - 1) * pitch[c]],
            send_sem=send_sem.at[5 + c], recv_sem=recv_sem.at[5 + c], device_id=(xn, py), device_id_type=MESH,
        ) for c in range(chunks)
    ]
    halo_wait = pltpu.make_async_remote_copy(
        src_ref=halo, dst_ref=halo, send_sem=send_sem.at[1], recv_sem=recv_sem.at[1],
        device_id=(xn, py), device_id_type=MESH,
    )
    rest = pots.at[0:py_size - 1, 4:16]
    pot_wait = pltpu.make_async_remote_copy(
        src_ref=rest, dst_ref=rest, send_sem=send_sem.at[2], recv_sem=recv_sem.at[2],
        device_id=(xn, py), device_id_type=MESH,
    )

    def turn_potential(x):
        flat_pots = pots.reshape(py_size * 16, 128)
        for y0 in range(0, 4, groups):
            loads = []
            for i in range(groups):
                if x == 0:
                    value = spans[0, pl.ds(per * 16 + y0 + i, py_size, stride=pitch[0]), :]
                else:
                    value = flat_pots[pl.ds(x * 4 + y0 + i, py_size, stride=16), :]
                value = (value - CENTRE) * SCALE
                loads += [value] * per
            pieces = turn_in(loads)
            for i in range(groups):
                diag[x, y0 + i] = pieces[i]

    for c in range(chunks):
        block_waits[c].wait_recv()
        for x in range(4):
            for y0 in range(0, 4, groups):
                pieces = turn_in([
                    states_of(spans.at[c], [s * 16 + x * 4 + y0 + i for s in range(per)], pitch[c])
                    for i in range(groups)
                ])
                for i in range(groups):
                    place(v0, c, x, y0 + i, pieces[i])
        if c == 0:
            halo_wait.wait_recv()
        for y0 in range(0, 4, groups):
            pieces = turn_in([
                states_of(halo, [(c * per + s) * 4 + y0 + i for s in range(per)], 8) for i in range(groups)
            ])
            for i in range(groups):
                place(v0, c, 4, y0 + i, pieces[i])
        apply(v0, c1, c)
        if c == 0:
            turn_potential(0)
        faces.append(send_faces(c1, v0, r1, c, 0))
    pot_wait.wait_recv()
    for x in (1, 2, 3):
        turn_potential(x)
    for c in range(chunks):
        for x in (1, 2, 3):
            for y in range(4):
                place(v1, c, x, y, 0.5 * folded(c1, v0, c, x, y))

    waiting = faces
    faces = []
    for c in range(chunks):
        for copy in waiting[c]:
            copy.wait_recv()
        for x, n in ((0, 0), (4, 1)):
            for y in range(4):
                place(v1, c, x, y, 0.5 * (c1[c, x, y] + r1[c, n, y]))
        apply(v1, c2, c)
        faces.append(send_faces(c2, v1, r2, c, 2))
    for c in range(chunks):
        for x in (1, 2, 3):
            for y in range(4):
                place(v2, c, x, y, folded(c2, v1, c, x, y) - v0[c, x, y])
    sent = waiting + faces

    def edge_copy(c, target):
        return send(
            block_of(send_edge.at[c], target, per * 4), block_of(edge, py * chunks + c, per * 4),
            5 + 2 * chunks + c, xn, target,
        )

    def back_copy(c, target):
        return send(
            block_of(send_back.at[c], target, per * 16), block_of(result, py * chunks + c, per * 16),
            5 + chunks + c, px, target,
        )

    waiting = faces
    for c in range(chunks):
        for copy in waiting[c]:
            copy.wait_recv()
        for x, n in ((0, 0), (4, 1)):
            for y in range(4):
                place(v2, c, x, y, c2[c, x, y] + r2[c, n, y] - v0[c, x, y])
        apply(v2, c3, c)
        for x in range(5):
            for y0 in range(0, 4, groups):
                values = []
                for i in range(groups):
                    value = folded(c3, v2, c, x, y0 + i)
                    if x < 4:
                        value = value - v1[c, x, y0 + i]
                    values.append(value)
                pieces = turn_out(values)
                for i in range(groups):
                    for s in range(per):
                        piece = pieces[i][s * py_size:(s + 1) * py_size]
                        if x < 4:
                            send_back[c, pl.ds(s * 16 + x * 4 + y0 + i, py_size, stride=per * 16), :] = piece
                        else:
                            send_edge[c, pl.ds(s * 4 + y0 + i, py_size, stride=per * 4), :] = piece

        over_all(functools.partial(edge_copy, c))
        over_others(functools.partial(back_copy, c))
        block_of(result, py * chunks + c, per * 16)[...] = block_of(send_back.at[c], py, per * 16)[...]

    edge_waits = [
        pltpu.make_async_remote_copy(
            src_ref=send_edge.at[c], dst_ref=edge.at[0:py_size * per * 4],
            send_sem=send_sem.at[5 + 2 * chunks + c], recv_sem=recv_sem.at[5 + 2 * chunks + c],
            device_id=(xn, py), device_id_type=MESH,
        ) for c in range(chunks)
    ]
    back_waits = [
        pltpu.make_async_remote_copy(
            src_ref=send_back.at[c, others], dst_ref=result.at[others],
            send_sem=send_sem.at[5 + chunks + c], recv_sem=recv_sem.at[5 + chunks + c],
            device_id=(xn, py), device_id_type=MESH,
        ) for c in range(chunks)
    ]
    for wait in edge_waits:
        wait.wait_recv()
    for wait in back_waits:
        wait.wait_recv()
    for s in range(own):
        for y in range(4):
            at = pl.ds(s * 16 + y, py_size, stride=own * 16)
            result[at, :] = result[at, :] + edge[pl.ds(s * 4 + y, py_size, stride=8), :]
    store = pltpu.make_async_copy(result, out_hbm, local_sem.at[0])
    store.start()
    for node in range(16):
        lhs[:, node * 128:(node + 1) * 128] = result[pl.ds(node, STATES, stride=16), :].astype(BF16)
    product = lax.dot_general(block_k[...], lhs[...], (((1,), (1,)), ((), ())), preferred_element_type=F32)
    for n in range(py_size):
        part[n // 16, n % 16, :, 0:STATES] = product[n * tile_cols:(n + 1) * tile_cols]

    def first_copy(target):
        return pltpu.make_async_remote_copy(
            src_ref=part.at[:, target], dst_ref=got1.at[plane], send_sem=send1, recv_sem=recv1,
            device_id=(px, z_part[0] + target), device_id_type=MESH,
        )

    for target in plane_group:
        first_copy(target).start()
    got1[plane] = part[:, plane]
    first_wait = pltpu.make_async_remote_copy(
        src_ref=got1.at[0:15], dst_ref=got1.at[0:15], send_sem=send1, recv_sem=recv1,
        device_id=(xn, py), device_id_type=MESH,
    )
    first_wait.wait_recv()
    total = got1[0]
    for n in range(1, 16):
        total = total + got1[n]
    sum1[...] = total

    def second_copy(x, z):
        return pltpu.make_async_remote_copy(
            src_ref=sum1.at[z], dst_ref=got2.at[px * 2 + z_own], send_sem=send2, recv_sem=recv2,
            device_id=(x, z * 16 + plane), device_id_type=MESH,
        )

    for x, z in column_group:
        second_copy(x, z).start()
    got2[px * 2 + z_own] = sum1[z_own]
    second_wait = pltpu.make_async_remote_copy(
        src_ref=got2.at[0:2 * px_size - 1], dst_ref=got2.at[0:2 * px_size - 1], send_sem=send2, recv_sem=recv2,
        device_id=(xn, py), device_id_type=MESH,
    )
    second_wait.wait_recv()
    total = got2[0]
    for n in range(1, 2 * px_size):
        total = total + got2[n]
    total = pltpu.roll(total, lax.rem(128 - px * tile_rows, 128), 1)
    total = jnp.concatenate([total, jnp.zeros((128 - tile_cols, 128), F32)], 0).T
    tile_ref[...] = total[0:tile_rows, 0:tile_cols]

    store.wait()
    for wait in block_waits + [halo_wait, pot_wait] + edge_waits + back_waits + [first_wait, second_wait]:
        wait.wait_send()
    for copies in sent:
        for copy in copies:
            copy.wait_send()


def local(px_size, py_size, span, potential, cell_matrix, block):
    chunks = CHUNKS
    own = STATES // py_size
    width = own // chunks * py_size
    rows = width
    field = pltpu.VMEM((chunks, 7, 5, rows, 128), F32)
    faces = pltpu.VMEM((chunks, 2, 4, rows, 128), F32)
    tile = (STATES // px_size, BLOCK // py_size)
    filtered, margin = pl.pallas_call(
        functools.partial(kernel, px_size, py_size, chunks),
        out_shape=(jax.ShapeDtypeStruct((STATES * 16, 128), F32), jax.ShapeDtypeStruct(tile, F32)),
        in_specs=[pl.BlockSpec(memory_space=pltpu.HBM)] * 4,
        out_specs=(pl.BlockSpec(memory_space=pl.ANY), pl.BlockSpec(memory_space=pltpu.VMEM)),
        scratch_shapes=[
            pltpu.VMEM((STATES * 16, 128), F32),
            pltpu.VMEM((py_size * (width // py_size * 16 + 4), 128), F32),
            pltpu.VMEM((125, 125), F32),
            pltpu.VMEM((128, 128), F32),
            pltpu.VMEM((BLOCK * 16, 128), BF16),
            pltpu.VMEM((BLOCK * 16, 128), F32),
            pltpu.VMEM((BLOCK, 2048), BF16),
            pltpu.VMEM((160, 480), BF16),
            pltpu.VMEM((4, 4, rows, 128), F32),
            pltpu.VMEM((chunks, py_size * (width // py_size * 16 + 4), 128), F32),
            pltpu.VMEM((py_size, 16, 128), F32),
            pltpu.VMEM((py_size * 8, 128), F32),
            pltpu.VMEM((py_size * 8, 128), F32),
            field, field, field, field, field, field, faces, faces,
            pltpu.VMEM((chunks, STATES * 16 // chunks, 128), F32),
            pltpu.VMEM((chunks, py_size * 8 // chunks, 128), F32),
            pltpu.VMEM((py_size * 8, 128), F32),
            pltpu.VMEM((STATES * 16, 128), F32),
            pltpu.VMEM((STATES, 2048), BF16),
            pltpu.VMEM((2, 16, tile[1], 128), F32),
            pltpu.VMEM((16, 2, tile[1], 128), F32),
            pltpu.VMEM((2, tile[1], 128), F32),
            pltpu.VMEM((2 * px_size, tile[1], 128), F32),
            pltpu.SemaphoreType.REGULAR,
            pltpu.SemaphoreType.DMA((4,)),
            pltpu.SemaphoreType.DMA((5 + 3 * chunks,)),
            pltpu.SemaphoreType.DMA((5 + 3 * chunks,)),
            pltpu.SemaphoreType.DMA((chunks, 4)),
            pltpu.SemaphoreType.DMA((chunks, 4)),
            pltpu.SemaphoreType.DMA,
            pltpu.SemaphoreType.DMA,
            pltpu.SemaphoreType.DMA,
            pltpu.SemaphoreType.DMA,
        ],
        compiler_params=pltpu.CompilerParams(
            collective_id=0, has_side_effects=True, vmem_limit_bytes=40 * 1024 * 1024
        ),
    )(*(pltpu.with_memory_space_constraint(value, pltpu.HBM) for value in (
        span.reshape(STATES * 16, 128), potential.reshape(16, 128), cell_matrix, block.reshape(BLOCK * 16, 128)
    )))
    return filtered.reshape(span.shape), margin


def solution(mesh):
    in_specs = (P(None, "px", "py", None), P("px", "py", None), P(), P(None, "px", "py", None))
    out_specs = (P(None, "px", "py", None), P("px", "py"))
    body = functools.partial(local, mesh.shape["px"], mesh.shape["py"])
    return jax.shard_map(body, mesh=mesh, in_specs=in_specs, out_specs=out_specs, check_vma=False)
```
